256 devices in a mesh: tile: 64 (over z, x, core), hour: 4 (over y).
Axes of the slice: x: 4, y: 4, z: 8, core: 2. Of those that a mesh axis runs over, the one named last changes fastest.
Arguments:
- spectra: float32 [32, 6, 1024, 512], P('hour', None, 'tile'), may hold values from -170 to 170
- send_list: int32 [64, 64, 2], P('tile'), may hold values from 0 to 16, as said below
- pair_list: int32 [64, 64, 2], P('tile'), may hold values from 0 to 127, as said below
- pair_count: int32 [64], P('tile'), may hold values from 1 to 64, as said below
Outputs:
- correlations: float32 [4096, 9216], P(('tile', 'hour'))
The draws below stay inside these ranges and needn't reach their ends.
Inputs may be any that keep to these rules, and one draw needn't show every extreme that they name: `send_list`: entries [o, t, :] name different stations of owner o's block; between 1 and 2 are used and come first, unused ones hold 16. Every owner fills its 2 slots for some tile, and one tile gets 2 stations from every owner. `pair_list`: slot o * 2 + j of tile t's pool holds the j-th station that owner o sends to t; each pair names two different used slots of its tile's pool. Only pairs p < pair_count[t] of tile t are live; some tile has all 64.
All inputs are finite; a program needn't handle non-finite values.
Results may differ from the reference program's by a relative error of at most 0.0003.
Values sent between devices are 32-bit elements; how exact they have to be, the bound alone decides.
A program may use at most 128 MiB of HBM per device.

```python
import math
import jax
import jax.numpy as jnp
from jax import lax

STB = 16
PMAX = 64
CAP = 2
F = 512
NFFT = 2048
LAGS = 1024
STATIONS = 1024
SEGS = 32
PAIRS = 4096
N_TILE = 64


def draw_spectra(key, part):
    key_base = jax.random.fold_in(key, 1)
    key_rough = jax.random.fold_in(key, 2)
    key_scale = jax.random.fold_in(key, 3)
    shape_full = (SEGS, 6, STATIONS, F)
    rough = jnp.exp(jax.random.uniform(key_rough, shape_full, jnp.float32, -1.2, 1.2))
    base = jnp.clip(jax.random.normal(key_base, shape_full, jnp.float32), -5.0, 5.0)
    station_scale = jnp.exp(jax.random.uniform(key_scale, (1, 1, STATIONS, 1), jnp.float32, 0.0, math.log(10.0)))
    return (base * rough * station_scale).astype(jnp.float32)


def routing(key):
    key_counts = jax.random.fold_in(key, 101)
    key_offset = jax.random.fold_in(key, 102)
    key_full = jax.random.fold_in(key, 103)
    key_orders = jax.random.fold_in(key, 104)
    key_first = jax.random.fold_in(key, 105)
    key_second = jax.random.fold_in(key, 106)
    positions = jnp.arange(N_TILE, dtype=jnp.int32)
    counts = jax.random.randint(key_counts, (N_TILE, N_TILE), 1, CAP + 1)
    offset = jax.random.randint(key_offset, (), 0, N_TILE)
    full_dest = jax.random.randint(key_full, (), 0, N_TILE)
    forced = (positions[None, :] == (positions[:, None] + offset) % N_TILE) | (positions[None, :] == full_dest)
    counts = jnp.where(forced, CAP, counts)
    orders = jax.vmap(lambda single: jax.random.permutation(single, STB))(jax.random.split(key_orders, N_TILE * N_TILE))
    orders = orders.reshape(N_TILE, N_TILE, STB)[:, :, :CAP]
    slot_index = jnp.arange(CAP, dtype=jnp.int32)
    sends = jnp.where(slot_index[None, None, :] < counts[:, :, None], orders, STB).astype(jnp.int32)
    valid_slot = (slot_index[None, None, :] < jnp.transpose(counts)[:, :, None]).reshape(N_TILE, CAP * N_TILE)
    scores = jnp.where(valid_slot, 0, CAP * N_TILE) + jnp.arange(CAP * N_TILE, dtype=jnp.int32)[None, :]
    ranked = jnp.argsort(scores, axis=1).astype(jnp.int32)
    live_total = jnp.sum(valid_slot.astype(jnp.int32), axis=1)
    first_pick = jax.random.randint(key_first, (N_TILE, PMAX), 0, live_total[:, None])
    step_pick = jax.random.randint(key_second, (N_TILE, PMAX), 0, live_total[:, None] - 1)
    second_pick = (first_pick + 1 + step_pick) % live_total[:, None]
    first_pick = first_pick.at[:, 0].set(live_total - 1)
    second_pick = second_pick.at[:, 0].set(0)
    pairings = jnp.stack([jnp.take_along_axis(ranked, first_pick, 1), jnp.take_along_axis(ranked, second_pick, 1)], -1)
    return (sends, pairings.astype(jnp.int32))


def draw_send_list(key, part):
    return routing(key)[0]


def draw_pair_list(key, part):
    return routing(key)[1]


def draw_pair_count(key, part):
    counts = jax.random.randint(jax.random.fold_in(key, 201), (N_TILE,), max(PMAX // 8, 1), PMAX // 2 + 1)
    busiest = jax.random.randint(jax.random.fold_in(key, 202), (), 0, N_TILE)
    return jnp.where(jnp.arange(N_TILE, dtype=jnp.int32) == busiest, PMAX, counts).astype(jnp.int32)


def setup_inputs(seed: int = 0) -> dict:
    key_of = jax.random.split(jax.random.key(seed), 5)
    return {
        "spectra": draw_spectra(jax.random.fold_in(key_of[4], 71), 0),
        "send_list": draw_send_list(jax.random.fold_in(key_of[4], 71), 0),
        "pair_list": draw_pair_list(jax.random.fold_in(key_of[4], 71), 0),
        "pair_count": draw_pair_count(jax.random.fold_in(key_of[4], 71), 0),
    }


def whiten(spectra):
    real_part = spectra[:, 0::2]
    imag_part = spectra[:, 1::2]
    power_sum = lax.optimization_barrier(jnp.sum(real_part * real_part + imag_part * imag_part, axis=1))
    bin_count = power_sum.shape[-1]
    padded = jnp.pad(power_sum, ((0, 0), (0, 0), (2, 2)))
    smoothed = (padded[..., 0:bin_count] + padded[..., 1:bin_count + 1] + padded[..., 2:bin_count + 2] + padded[..., 3:bin_count + 3] + padded[..., 4:bin_count + 4]) / 15.0
    water_level = lax.optimization_barrier(jnp.sum(power_sum, axis=-1, keepdims=True)) / (3.0 * bin_count)
    return spectra / jnp.sqrt(smoothed + 0.25 * water_level + 1e-06)[:, None]

def cross_spectra(first_rows, second_rows):
    first_real = first_rows[..., 0::2, :, :]
    first_imag = first_rows[..., 1::2, :, :]
    second_real = second_rows[..., 0::2, :, :]
    second_imag = second_rows[..., 1::2, :, :]
    real_part = first_real[..., :, None, :, :] * second_real[..., None, :, :, :] + first_imag[..., :, None, :, :] * second_imag[..., None, :, :, :]
    imag_part = first_imag[..., :, None, :, :] * second_real[..., None, :, :, :] - first_real[..., :, None, :, :] * second_imag[..., None, :, :, :]
    return jnp.stack([real_part, imag_part], axis=-3)

def lag_table(bin_count, lag_count, length, segment_total):
    frequency = jnp.arange(bin_count, dtype=jnp.int32)
    lag_index = jnp.arange(lag_count, dtype=jnp.int32) - lag_count // 2
    phases = jnp.mod(frequency[:, None] * lag_index[None, :], length).astype(jnp.float32) * (2.0 * math.pi / length)
    normalizer = 1.0 / math.sqrt(bin_count * segment_total)
    return jnp.stack([jnp.cos(phases) * normalizer, -jnp.sin(phases) * normalizer])

def reference(spectra, send_list, pair_list, pair_count):
    whitened = whiten(spectra)
    weights_table = lag_table(F, LAGS, NFFT, SEGS)
    owner_base = jnp.arange(N_TILE, dtype=jnp.int32)[:, None] * STB
    slot_numbers = jnp.arange(PMAX, dtype=jnp.int32)

    def per_tile(tile_index):
        picked = lax.dynamic_index_in_dim(send_list, tile_index, 1, keepdims=False)
        used_mask = picked < STB
        station_index = jnp.where(used_mask, owner_base + picked, 0).reshape(-1)
        used_scale = used_mask.reshape(-1).astype(jnp.float32)
        pair_rows = lax.dynamic_index_in_dim(pair_list, tile_index, 0, keepdims=False)
        first_slot = pair_rows[:, 0]
        second_slot = pair_rows[:, 1]
        first_rows = jnp.take(whitened, station_index[first_slot], axis=2) * used_scale[first_slot][:, None]
        second_rows = jnp.take(whitened, station_index[second_slot], axis=2) * used_scale[second_slot][:, None]
        spectral_sum = lax.optimization_barrier(jnp.sum(cross_spectra(first_rows, second_rows), axis=0)).reshape(9, 2, PMAX, F)
        live_mask = (slot_numbers < pair_count[tile_index]).astype(jnp.float32)
        spectral_sum = spectral_sum * live_mask[:, None]
        lagged = jnp.einsum('csqf,sfl->qcl', spectral_sum, weights_table, precision=lax.Precision.HIGHEST)
        return lagged.reshape(PMAX, 9 * LAGS)
    return lax.map(per_tile, jnp.arange(N_TILE, dtype=jnp.int32)).reshape(PAIRS, 9 * LAGS)
```

```python
import functools
import math

import jax
import jax.numpy as jnp
from jax import lax
from jax.experimental import pallas as pl
from jax.experimental.pallas import tpu as pltpu
from jax.sharding import PartitionSpec as P

MESH = pl.DeviceIdType.MESH
F32, BF16, I32 = jnp.float32, jnp.bfloat16, jnp.int32

NFFT = 2048
LAGS = 1024
BINS = 512
SEGS = 32
HS = 8
STB = 16
NT, NH = 64, 4
ND = NT * NH
CH = 12
RR = 5


def position():
    t = lax.axis_index("tile")
    return t, lax.axis_index("hour"), t // 8, t % 8


def entry_barrier(signal_only=False):
    t, h, z, xc = position()
    bar = pltpu.get_barrier_semaphore()
    for i in range(1, 8):
        pl.semaphore_signal(bar, inc=1, device_id=(((z + i) % 8) * 8 + xc, h), device_id_type=MESH)
    for i in range(1, 8):
        pl.semaphore_signal(bar, inc=1, device_id=(z * 8 + (xc + i) % 8, h), device_id_type=MESH)
    for i in range(1, NH):
        pl.semaphore_signal(bar, inc=1, device_id=(t, (h + i) % NH), device_id_type=MESH)


def entry_barrier_rest(plane_sem, all_sem):
    t, h, z, xc = position()
    pl.semaphore_wait(pltpu.get_barrier_semaphore(), 17)
    for i in range(1, 8):
        pl.semaphore_signal(plane_sem, inc=1, device_id=(z * 8 + (xc + i) % 8, h), device_id_type=MESH)
    pl.semaphore_wait(plane_sem, 7)
    for i in range(1, NH):
        pl.semaphore_signal(all_sem, inc=1, device_id=(t, (h + i) % NH), device_id_type=MESH)
    pl.semaphore_wait(all_sem, NH - 1)


def peer(i):
    t, h, z, xc = position()
    x, c = xc // 2, xc % 2
    z2 = (z + (i // 2) % 8) % 8
    x2 = (x + (i // 16) % 4) % 4
    c2 = (c + i) % 2
    return (z2 * 4 + x2) * 2 + c2, (h + i // 64) % NH


def roll(x, shift, axis):
    return pltpu.roll(x, shift, axis)


def swap_blocks(x):
    sub = lax.broadcasted_iota(I32, (8, 128), 0)
    lane = lax.broadcasted_iota(I32, (8, 128), 1)
    for b in (1, 2, 4):
        step = 16 * b
        sb = (sub & b) != 0
        lb = (lane & step) != 0
        down = roll(roll(x, 8 - b, 0), step, 1)
        up = roll(roll(x, b, 0), 128 - step, 1)
        x = jnp.where(sb == lb, x, jnp.where(sb, up, down))
    return x


def spread_kernel(spec_ref, lists_ref, recv_ref, lout_ref, white, pack, plane_sem, all_sem, send_sem, recv_sem,
                  lsend_sem, lrecv_sem, loc_sem, lloc_sem):
    t, h, _, _ = position()
    entry_barrier()
    lane = lax.broadcasted_iota(I32, (STB, BINS), 1)

    def whiten(s, carry):
        x = spec_ref[s]
        power = jnp.sum(x * x, axis=0)
        total = power
        total += jnp.where(lane >= 1, roll(power, 1, 1), 0.0)
        total += jnp.where(lane >= 2, roll(power, 2, 1), 0.0)
        total += jnp.where(lane < BINS - 1, roll(power, BINS - 1, 1), 0.0)
        total += jnp.where(lane < BINS - 2, roll(power, BINS - 2, 1), 0.0)
        water = jnp.sum(power, axis=1, keepdims=True) * (1.0 / (3.0 * BINS))
        inv = 1.0 / jnp.sqrt(total * (1.0 / 15.0) + 0.25 * water + 1e-06)
        white[:, pl.ds(pl.multiple_of(s * STB, STB), STB), :] = x * inv[None]
        return carry

    lax.fori_loop(0, HS, whiten, 0)
    for c in range(6):
        for kb in range(4):
            block = white[c, :, kb * 128:(kb + 1) * 128].T
            pack[pl.ds((kb % 2) * 128, 128), (kb // 2) * 6 + c, :] = block
    entry_barrier_rest(plane_sem, all_sem)
    me = t * NH + h
    own = pltpu.make_async_copy(pack.at[h * NT + t], recv_ref.at[me], loc_sem)
    own.start()
    lown = pltpu.make_async_copy(lists_ref, lout_ref.at[t], lloc_sem)
    lown.start()

    def send_lists(i, carry):
        t2, _ = peer(i)
        pltpu.make_async_remote_copy(src_ref=lists_ref, dst_ref=lout_ref.at[t], send_sem=lsend_sem,
                                     recv_sem=lrecv_sem, device_id=(t2, h), device_id_type=MESH).start()
        return carry

    def send(i, carry):
        t2, h2 = peer(i)
        pltpu.make_async_remote_copy(src_ref=pack.at[h2 * NT + t2], dst_ref=recv_ref.at[me], send_sem=send_sem,
                                     recv_sem=recv_sem, device_id=(t2, h2), device_id_type=MESH).start()
        return carry

    lax.fori_loop(1, ND, send, 0)
    lax.fori_loop(1, NT, send_lists, 0)
    own.wait()
    lown.wait()
    rest, lrest = pl.ds(0, ND - 1), pl.ds(0, NT - 1)
    pltpu.make_async_copy(pack.at[rest], pack.at[rest], send_sem).wait()
    pltpu.make_async_copy(recv_ref.at[rest], recv_ref.at[rest], recv_sem).wait()
    pltpu.make_async_copy(lout_ref.at[lrest], lout_ref.at[lrest], lsend_sem).wait()
    pltpu.make_async_copy(lout_ref.at[lrest], lout_ref.at[lrest], lrecv_sem).wait()


def spread(spectra, lists):
    vmem = pl.BlockSpec(memory_space=pltpu.VMEM)
    sem = pltpu.SemaphoreType
    return pl.pallas_call(
        spread_kernel,
        out_shape=(jax.ShapeDtypeStruct((ND, CH, 128), F32), jax.ShapeDtypeStruct((NT, 2, 128), I32)),
        in_specs=[vmem, vmem],
        out_specs=(vmem, vmem),
        scratch_shapes=[pltpu.VMEM((6, HS * STB, BINS), F32), pltpu.VMEM((ND, CH, 128), F32),
                        sem.REGULAR, sem.REGULAR] + [sem.DMA] * 6,
        compiler_params=pltpu.CompilerParams(collective_id=0, has_side_effects=True),
        name="spread",
    )(spectra, lists)


def resolve_stations(lout_ref, slots_ref, idx_ref):
    sends = lout_ref[:, 0, :].astype(F32)
    slots_ref[...] = jnp.concatenate([sends, jnp.zeros((64, 128), F32)], axis=0).T
    first = slots_ref[pl.ds(0, NT, stride=2), :]
    second = slots_ref[pl.ds(1, NT, stride=2), :]
    slot = lout_ref[:, 1, :]
    owner = jnp.maximum(slot, 0) // 2
    pick = jnp.where(slot % 2 == 0, jnp.take_along_axis(first, owner, axis=1),
                     jnp.take_along_axis(second, owner, axis=1))
    station = owner.astype(F32) * STB + pick
    station = jnp.where((slot < 0) | (pick >= STB), -1.0, station)
    for tg in range(8):
        idx_ref[tg] = swap_blocks(station[tg * 8:(tg + 1) * 8])


def build_table(recv_ref, table_ref):
    sub = lax.broadcasted_iota(I32, (8, 128), 0)
    lane = lax.broadcasted_iota(I32, (8, 128), 1)
    l16, l32, l64 = (lane & 16) != 0, (lane & 32) != 0, (lane & 64) != 0
    same, top = ((sub & 4) != 0) == l16, (sub & 4) != 0

    def group(og, carry):
        for f in range(2):
            for ci in range(3):
                parts = []
                for c in (2 * ci, 2 * ci + 1):
                    v = []
                    for g in range(4):
                        x = recv_ref[pl.ds(og * 32 + g * 8, 8), f * 6 + c, :]
                        y = roll(x, 4, 0)
                        v.append(jnp.where(same, x, jnp.where(top, roll(y, 112, 1), roll(y, 16, 1))))
                    w = [None] * 4
                    for hi in range(2):
                        a, b = v[2 * hi], v[2 * hi + 1]
                        w[2 * hi] = jnp.where(l32, roll(b, 32, 1), a)
                        w[2 * hi + 1] = jnp.where(l32, b, roll(a, 96, 1))
                    u = [None] * 4
                    for lo in range(2):
                        a, b = w[lo], w[2 + lo]
                        u[lo] = jnp.where(l64, roll(b, 64, 1), a)
                        u[2 + lo] = jnp.where(l64, b, roll(a, 64, 1))
                    parts.append(u)
                for sv in range(4):
                    both = jnp.concatenate([parts[0][sv], parts[1][sv]], axis=0)
                    high = both.astype(BF16)
                    low = (both - high.astype(F32)).astype(BF16)
                    row = ((sv * 2 + f) * 6 + 2 * ci) * 8
                    cols = pl.ds(pl.multiple_of(og * 128, 128), 128)
                    table_ref[row:row + 16, cols] = high
                    table_ref[384 + row:384 + row + 16, cols] = low
        return carry

    lax.fori_loop(0, 8, group, 0)


def pair_kernel(recv_ref, lout_ref, out_ref, slots_ref, idx_ref, table_ref, prod_ref):
    resolve_stations(lout_ref, slots_ref, idx_ref)
    build_table(recv_ref, table_ref)
    station = lax.broadcasted_iota(I32, (1024, 256), 0)

    def block(i, carry):
        tg, h = i // NH, i % NH
        wanted = jnp.concatenate([idx_ref[tg, pl.ds(h, 1), :], idx_ref[tg, pl.ds(4 + h, 1), :]], axis=1)
        live = jnp.max(wanted) >= 0.0
        rows = pl.ds(h * NT + tg * 8, 8)

        @pl.when(live)
        def _():
            chosen = (station == wanted.astype(I32)).astype(F32).astype(BF16)
            full = jnp.dot(table_ref[...], chosen, preferred_element_type=F32)
            prod_ref[...] = full[:384] + full[384:]
            sums = {}
            for f in range(2):
                acc = [None] * 18
                for sv in range(4):
                    base = (sv * 2 + f) * 48
                    a = [prod_ref[base + 8 * c:base + 8 * c + 8, 0:128] for c in range(6)]
                    b = [prod_ref[base + 8 * c:base + 8 * c + 8, 128:256] for c in range(6)]
                    for p in range(3):
                        for q in range(3):
                            re = a[2 * p] * b[2 * q] + a[2 * p + 1] * b[2 * q + 1]
                            im = a[2 * p + 1] * b[2 * q] - a[2 * p] * b[2 * q + 1]
                            n = (p * 3 + q) * 2
                            acc[n] = re if sv == 0 else acc[n] + re
                            acc[n + 1] = im if sv == 0 else acc[n + 1] + im
                for n in range(18):
                    sums[n * 2 + f] = jnp.sum(acc[n], axis=0, keepdims=True)
            for r in range(RR):
                got = [sums.get(r * 8 + g) for g in range(8)]
                got = [jnp.zeros((1, 128), F32) if v is None else v for v in got]
                out_ref[rows, r, :] = swap_blocks(jnp.concatenate(got, axis=0))

        @pl.when(jnp.logical_not(live))
        def _():
            out_ref[rows, :, :] = jnp.zeros((8, RR, 128), F32)

        return carry

    lax.fori_loop(0, 32, block, 0)


def pair_products(received, lists):
    vmem = pl.BlockSpec(memory_space=pltpu.VMEM)
    return pl.pallas_call(
        pair_kernel,
        out_shape=jax.ShapeDtypeStruct((ND, RR, 128), F32),
        in_specs=[vmem, vmem],
        out_specs=vmem,
        scratch_shapes=[pltpu.VMEM((128, 128), F32), pltpu.VMEM((8, 8, 128), F32), pltpu.VMEM((768, 1024), BF16),
                        pltpu.VMEM((384, 256), F32)],
        name="pair_products",
    )(received, lists)


def lag_tables(high_ref, low_ref, fine_ref):
    scale = 1.0 / math.sqrt(BINS * SEGS)
    lag = lax.broadcasted_iota(I32, (32, LAGS), 1) - LAGS // 2
    fine = ((lax.broadcasted_iota(I32, (32, LAGS), 0) * lag) & (NFFT - 1)).astype(F32) * (2.0 * math.pi / NFFT)
    fine_ref[0] = jnp.cos(fine)
    fine_ref[1] = jnp.sin(fine)
    lag1 = lax.broadcasted_iota(I32, (8, LAGS), 1) - LAGS // 2

    def rows(a, carry):
        coarse = ((lag1 * (32 * a)) & (NFFT - 1)).astype(F32) * (2.0 * math.pi / NFFT)
        cosine, sine = jnp.cos(coarse)[0:1] * scale, jnp.sin(coarse)[0:1] * scale
        at = pl.multiple_of(a * 32, 32)
        for part, value in ((0, cosine * fine_ref[0] - sine * fine_ref[1]),
                            (BINS, -(sine * fine_ref[0] + cosine * fine_ref[1]))):
            high = value.astype(BF16)
            high_ref[pl.ds(part + at, 32), :] = high
            low_ref[pl.ds(part + at, 32), :] = (value - high.astype(F32)).astype(BF16)
        return carry

    lax.fori_loop(0, BINS // 32, rows, 0)


def collect_kernel(cross_ref, out_ref, recv, high_ref, low_ref, fine_ref, sum_ref, plane_sem, all_sem, send_sem,
                   recv_sem, loc_sem):
    t, h, _, _ = position()
    entry_barrier()
    me = h * NT + t
    entry_barrier_rest(plane_sem, all_sem)
    own = pltpu.make_async_copy(cross_ref.at[me], recv.at[me], loc_sem)
    own.start()

    def send(i, carry):
        t2, h2 = peer(i)
        pltpu.make_async_remote_copy(src_ref=cross_ref.at[h2 * NT + t2], dst_ref=recv.at[me], send_sem=send_sem,
                                     recv_sem=recv_sem, device_id=(t2, h2), device_id_type=MESH).start()
        return carry

    lax.fori_loop(1, ND, send, 0)
    lag_tables(high_ref, low_ref, fine_ref)
    own.wait()
    rest = pl.ds(0, ND - 1)
    pltpu.make_async_copy(cross_ref.at[rest], cross_ref.at[rest], send_sem).wait()
    pltpu.make_async_copy(recv.at[rest], recv.at[rest], recv_sem).wait()
    for r in range(RR):
        turned = recv[:, r, :].T
        for g in range(8):
            m = r * 8 + g
            if m < 36:
                sum_ref[(m // 4) * 16:(m // 4) * 16 + 16, (m % 4) * 256:(m % 4) * 256 + 256] = turned[g * 16:g * 16 + 16]
    total = sum_ref[...]
    high = total.astype(BF16)
    low = (total - high.astype(F32)).astype(BF16)
    for j in range(4):
        cols = slice(j * 256, j * 256 + 256)
        part = jnp.dot(high, high_ref[:, cols], preferred_element_type=F32)
        part += jnp.dot(high, low_ref[:, cols], preferred_element_type=F32)
        part += jnp.dot(low, high_ref[:, cols], preferred_element_type=F32)
        for c in range(9):
            out_ref[:, c * LAGS + j * 256:c * LAGS + j * 256 + 256] = part[c * 16:c * 16 + 16]


def collect(cross):
    vmem = pl.BlockSpec(memory_space=pltpu.VMEM)
    sem = pltpu.SemaphoreType
    return pl.pallas_call(
        collect_kernel,
        out_shape=jax.ShapeDtypeStruct((16, 9 * LAGS), F32),
        in_specs=[vmem],
        out_specs=vmem,
        scratch_shapes=[pltpu.VMEM((ND, RR, 128), F32), pltpu.VMEM((2 * BINS, LAGS), BF16),
                        pltpu.VMEM((2 * BINS, LAGS), BF16), pltpu.VMEM((2, 32, LAGS), F32),
                        pltpu.VMEM((144, 2 * BINS), F32), sem.REGULAR, sem.REGULAR, sem.DMA, sem.DMA, sem.DMA],
        compiler_params=pltpu.CompilerParams(collective_id=1, has_side_effects=True),
        name="collect",
    )(cross)


def body(spectra, send_list, pair_list, pair_count):
    pairs = pair_list[0]
    live = jnp.arange(pairs.shape[0], dtype=I32)[:, None] < pair_count[0]
    slots = jnp.where(live, pairs, -1).T.reshape(128)
    lists = jnp.stack([send_list[0].reshape(128), slots])
    received, all_lists = spread(spectra, lists)
    return collect(pair_products(received, all_lists))


def solution(mesh):
    in_specs = (P("hour", None, "tile", None), P("tile", None, None), P("tile", None, None), P("tile"))
    return jax.shard_map(body, mesh=mesh, in_specs=in_specs, out_specs=P(("tile", "hour"), None), check_vma=False)
```

```python
import functools
import math

import jax
import jax.numpy as jnp
from jax import lax
from jax.experimental import pallas as pl
from jax.experimental.pallas import tpu as pltpu
from jax.sharding import PartitionSpec as P

MESH = pl.DeviceIdType.MESH
F32, BF16, I32 = jnp.float32, jnp.bfloat16, jnp.int32

NFFT = 2048
LAGS = 1024
BINS = 512
SEGS = 32
HS = 8
STB = 16
NT, NH = 64, 4
ND = NT * NH
CH = 12
RR = 5


def position():
    t = lax.axis_index("tile")
    return t, lax.axis_index("hour"), t // 8, t % 8


def entry_barrier(signal_only=False):
    t, h, z, xc = position()
    bar = pltpu.get_barrier_semaphore()
    for i in range(1, 8):
        pl.semaphore_signal(bar, inc=1, device_id=(((z + i) % 8) * 8 + xc, h), device_id_type=MESH)
    for i in range(1, 8):
        pl.semaphore_signal(bar, inc=1, device_id=(z * 8 + (xc + i) % 8, h), device_id_type=MESH)
    for i in range(1, NH):
        pl.semaphore_signal(bar, inc=1, device_id=(t, (h + i) % NH), device_id_type=MESH)


def entry_barrier_rest(plane_sem, all_sem):
    t, h, z, xc = position()
    pl.semaphore_wait(pltpu.get_barrier_semaphore(), 17)
    for i in range(1, 8):
        pl.semaphore_signal(plane_sem, inc=1, device_id=(z * 8 + (xc + i) % 8, h), device_id_type=MESH)
    pl.semaphore_wait(plane_sem, 7)
    for i in range(1, NH):
        pl.semaphore_signal(all_sem, inc=1, device_id=(t, (h + i) % NH), device_id_type=MESH)
    pl.semaphore_wait(all_sem, NH - 1)


def each_peer(planes, act):
    t, h, z, xc = position()
    zs = [((z + d) % 8) * 8 for d in range(8)]
    cs = [(xc + d) % 2 for d in range(2)]

    def some(k, carry):
        x2, h2 = ((xc // 2 + k) % 4) * 2, (h + k // 4) % NH
        for dz in range(8):
            for dc in range(2):
                if dz + dc == 0:
                    pl.when(k > 0)(lambda: act(zs[0] + x2 + cs[0], h2))
                else:
                    act(zs[dz] + x2 + cs[dc], h2)
        return carry

    lax.fori_loop(0, 4 * planes, some, 0)


def roll(x, shift, axis):
    return pltpu.roll(x, shift, axis)


def swap_blocks(x):
    sub = lax.broadcasted_iota(I32, (8, 128), 0)
    lane = lax.broadcasted_iota(I32, (8, 128), 1)
    for b in (1, 2, 4):
        step = 16 * b
        sb = (sub & b) != 0
        lb = (lane & step) != 0
        down = roll(roll(x, 8 - b, 0), step, 1)
        up = roll(roll(x, b, 0), 128 - step, 1)
        x = jnp.where(sb == lb, x, jnp.where(sb, up, down))
    return x


def lag_tables(high_ref, low_ref, fine_ref):
    scale = 1.0 / math.sqrt(BINS * SEGS)
    lag = lax.broadcasted_iota(I32, (32, LAGS), 1) - LAGS // 2
    fine = ((lax.broadcasted_iota(I32, (32, LAGS), 0) * lag) & (NFFT - 1)).astype(F32) * (2.0 * math.pi / NFFT)
    fine_ref[0] = jnp.cos(fine)
    fine_ref[1] = jnp.sin(fine)
    lag1 = lax.broadcasted_iota(I32, (8, LAGS), 1) - LAGS // 2

    def rows(a, carry):
        coarse = ((lag1 * (32 * a)) & (NFFT - 1)).astype(F32) * (2.0 * math.pi / NFFT)
        cosine, sine = jnp.cos(coarse)[0:1] * scale, jnp.sin(coarse)[0:1] * scale
        at = pl.multiple_of(a * 32, 32)
        for part, value in ((0, cosine * fine_ref[0] - sine * fine_ref[1]),
                            (BINS, -(sine * fine_ref[0] + cosine * fine_ref[1]))):
            high = value.astype(BF16)
            high_ref[pl.ds(part + at, 32), :] = high
            low_ref[pl.ds(part + at, 32), :] = (value - high.astype(F32)).astype(BF16)
        return carry

    lax.fori_loop(0, BINS // 32, rows, 0)


def whiten_all(spec_ref, white):
    lane = lax.broadcasted_iota(I32, (STB, BINS), 1)

    def one(s, carry):
        x = spec_ref[s]
        power = jnp.sum(x * x, axis=0)
        total = power
        total += jnp.where(lane >= 1, roll(power, 1, 1), 0.0)
        total += jnp.where(lane >= 2, roll(power, 2, 1), 0.0)
        total += jnp.where(lane < BINS - 1, roll(power, BINS - 1, 1), 0.0)
        total += jnp.where(lane < BINS - 2, roll(power, BINS - 2, 1), 0.0)
        water = jnp.sum(power, axis=1, keepdims=True) * (1.0 / (3.0 * BINS))
        inv = 1.0 / jnp.sqrt(total * (1.0 / 15.0) + 0.25 * water + 1e-06)
        white[:, pl.ds(pl.multiple_of(s * STB, STB), STB), :] = x * inv[None]
        return carry

    lax.fori_loop(0, HS, one, 0)


def pack_bin(f, white, pack):
    for c in range(6):
        for half in range(2):
            cols = slice((2 * f + half) * 128, (2 * f + half) * 128 + 128)
            pack[f, pl.ds(half * 1024 + c, 128, stride=8), :] = white[c, :, cols].T


def resolve_stations(lout_ref, slots_ref, idx_ref):
    sends = lout_ref[:, 0, :].astype(F32)
    slots_ref[...] = jnp.concatenate([sends, jnp.zeros((64, 128), F32)], axis=0).T
    first = slots_ref[pl.ds(0, NT, stride=2), :]
    second = slots_ref[pl.ds(1, NT, stride=2), :]
    slot = lout_ref[:, 1, :]
    owner = jnp.maximum(slot, 0) // 2
    pick = jnp.where(slot % 2 == 0, jnp.take_along_axis(first, owner, axis=1),
                     jnp.take_along_axis(second, owner, axis=1))
    station = owner.astype(F32) * STB + pick
    station = jnp.where((slot < 0) | (pick >= STB), -1.0, station)
    for tg in range(8):
        idx_ref[tg] = swap_blocks(station[tg * 8:(tg + 1) * 8])


def build_selectors(idx_ref, hot):
    station = lax.broadcasted_iota(I32, (128, 256), 0)

    def one(i, carry):
        tg, h = i // NH, i % NH
        wanted = jnp.concatenate([idx_ref[tg, pl.ds(h, 1), :], idx_ref[tg, pl.ds(4 + h, 1), :]], axis=1).astype(I32)
        for k in range(8):
            hot[i, k * 128:k * 128 + 128, :] = (station == wanted - k * 128).astype(F32).astype(BF16)
        return carry

    lax.fori_loop(0, 32, one, 0)


def build_table(f, recv, table):
    sub = lax.broadcasted_iota(I32, (8, 128), 0)
    lane = lax.broadcasted_iota(I32, (8, 128), 1)
    l16, l32, l64 = (lane & 16) != 0, (lane & 32) != 0, (lane & 64) != 0
    same, top = ((sub & 4) != 0) == l16, (sub & 4) != 0

    def group(og, carry):
        for ci in range(3):
            parts = []
            for c in (2 * ci, 2 * ci + 1):
                v = []
                for g in range(4):
                    x = recv[f, pl.ds(og * 256 + g * 64 + c, 8, stride=8), :]
                    y = roll(x, 4, 0)
                    v.append(jnp.where(same, x, jnp.where(top, roll(y, 112, 1), roll(y, 16, 1))))
                w = [None] * 4
                for hi in range(2):
                    a, b = v[2 * hi], v[2 * hi + 1]
                    w[2 * hi] = jnp.where(l32, roll(b, 32, 1), a)
                    w[2 * hi + 1] = jnp.where(l32, b, roll(a, 96, 1))
                u = [None] * 4
                for lo in range(2):
                    a, b = w[lo], w[2 + lo]
                    u[lo] = jnp.where(l64, roll(b, 64, 1), a)
                    u[2 + lo] = jnp.where(l64, b, roll(a, 64, 1))
                parts.append(u)
            for sv in range(4):
                both = jnp.concatenate([parts[0][sv], parts[1][sv]], axis=0)
                high = both.astype(BF16)
                low = (both - high.astype(F32)).astype(BF16)
                row = (sv * 6 + 2 * ci) * 8
                cols = pl.ds(pl.multiple_of(og * 128, 128), 128)
                table[row:row + 16, cols] = high
                table[192 + row:192 + row + 16, cols] = low
        return carry

    lax.fori_loop(0, 8, group, 0)


def pair_sums(table, chosen, prod):
    full = jnp.dot(table[...], chosen, preferred_element_type=F32)
    prod[...] = full[:192] + full[192:]
    acc = [None] * 18
    for sv in range(4):
        rows = [slice((sv * 6 + c) * 8, (sv * 6 + c) * 8 + 8) for c in range(6)]
        a = [prod[r, 0:128] for r in rows]
        b = [prod[r, 128:256] for r in rows]
        for p in range(3):
            for q in range(3):
                re = a[2 * p] * b[2 * q] + a[2 * p + 1] * b[2 * q + 1]
                im = a[2 * p + 1] * b[2 * q] - a[2 * p] * b[2 * q + 1]
                n = (p * 3 + q) * 2
                acc[n] = re if sv == 0 else acc[n] + re
                acc[n + 1] = im if sv == 0 else acc[n + 1] + im
    return [jnp.sum(v, axis=0, keepdims=True) for v in acc]


def block_at(i):
    _, h, z, _ = position()
    return (z + 3 * (i + 1)) % 8, (h + i // 8 + 1) % NH


def correlate_kernel(spec_ref, lists_ref, out_ref, white, pack, recv, lout, slots_ref, idx_ref, hot, table, prod, half,
                     cross, got, high_ref, low_ref, fine_ref, sum_ref, plane_sem, all_sem, send_sem, recv_sem, own_sem,
                     lsend_sem, lrecv_sem, lown_sem, osend_sem, orecv_sem, oown_sem):
    t, h, _, _ = position()
    me, mine = t * NH + h, h * NT + t
    entry_barrier()
    whiten_all(spec_ref, white)
    pack_bin(0, white, pack)
    entry_barrier_rest(plane_sem, all_sem)

    def rows_of(d, n):
        return pl.ds(pl.multiple_of(d * 8, 8), n)

    def send_lists(t2, h2):
        pltpu.make_async_remote_copy(src_ref=lists_ref, dst_ref=lout.at[t], send_sem=lsend_sem, recv_sem=lrecv_sem,
                                     device_id=(t2, h2), device_id_type=MESH).start()

    each_peer(1, send_lists)
    lown = pltpu.make_async_copy(lists_ref, lout.at[t], lown_sem)
    lown.start()
    owns = []
    for f in range(2):
        def send(t2, h2, f=f):
            pltpu.make_async_remote_copy(src_ref=pack.at[f, rows_of(h2 * NT + t2, 6)], dst_ref=recv.at[f, rows_of(me, 6)],
                                         send_sem=send_sem.at[f], recv_sem=recv_sem.at[f], device_id=(t2, h2),
                                         device_id_type=MESH).start()

        if f == 1:
            pack_bin(1, white, pack)
        own = pltpu.make_async_copy(pack.at[f, rows_of(mine, 6)], recv.at[f, rows_of(me, 6)], own_sem.at[f])
        own.start()
        owns.append(own)
        each_peer(NH, send)
    lown.wait()
    lrest = pl.ds(0, NT - 1)
    pltpu.make_async_copy(lout.at[lrest], lout.at[lrest], lrecv_sem).wait()
    resolve_stations(lout, slots_ref, idx_ref)
    build_selectors(idx_ref, hot)
    lag_tables(high_ref, low_ref, fine_ref)
    rest = pl.ds(0, (ND - 1) * 6)

    def arrived(f):
        owns[f].wait()
        pltpu.make_async_copy(recv.at[f, rest], recv.at[f, rest], recv_sem.at[f]).wait()
        build_table(f, recv, table)

    arrived(0)

    def first(k, carry):
        for j in range(2):
            i = 2 * k + j
            sums = pair_sums(table, hot[i], prod.at[j])
            half[i, 0:18, :] = jnp.concatenate(sums, axis=0)
        return carry

    lax.fori_loop(0, 16, first, 0)
    arrived(1)

    def deliver(i):
        tg, h2 = block_at(i)
        for x in range(8):
            t2 = tg * 8 + x
            src, dst = cross.at[rows_of(h2 * NT + t2, RR)], got.at[rows_of(mine, RR)]

            @pl.when(h2 * NT + t2 != mine)
            def _():
                pltpu.make_async_remote_copy(src_ref=src, dst_ref=dst, send_sem=osend_sem, recv_sem=orecv_sem,
                                             device_id=(t2, h2), device_id_type=MESH).start()

            @pl.when(h2 * NT + t2 == mine)
            def _():
                pltpu.make_async_copy(src, dst, oown_sem).start()

    def second(k, carry):
        for j in range(2):
            i = 2 * k + j
            tg, h2 = block_at(i)
            sums = pair_sums(table, hot[tg * NH + h2], prod.at[j])
            before = half[tg * NH + h2]
            zero = jnp.zeros((4, 128), F32)
            parts = [before[0:8], before[8:16], jnp.concatenate([before[16:18]] + sums[0:6], axis=0),
                     jnp.concatenate(sums[6:14], axis=0), jnp.concatenate(sums[14:18] + [zero], axis=0)]
            for r in range(RR):
                cross[pl.ds((h2 * NT + tg * 8) * 8 + r, 8, stride=8), :] = swap_blocks(parts[r])
        for j in range(2):
            deliver(2 * k + j)
        return carry

    lax.fori_loop(0, 16, second, 0)
    pltpu.make_async_copy(cross.at[mine_rows(mine)], got.at[mine_rows(mine)], oown_sem).wait()
    orest = pl.ds(0, (ND - 1) * RR)
    pltpu.make_async_copy(got.at[orest], got.at[orest], orecv_sem).wait()
    for r in range(RR):
        turned = got[pl.ds(r, ND, stride=8), :].T
        for g in range(8):
            m = r * 8 + g
            if m < 36:
                f, c, ri = m // 18, m % 18 // 2, m % 2
                at = (ri * 2 + f) * 256
                sum_ref[c * 16:c * 16 + 16, at:at + 256] = turned[g * 16:g * 16 + 16]
    total = sum_ref[...]
    high = total.astype(BF16)
    low = (total - high.astype(F32)).astype(BF16)
    for j in range(4):
        cols = slice(j * 256, j * 256 + 256)
        part = jnp.dot(high, high_ref[:, cols], preferred_element_type=F32)
        part += jnp.dot(high, low_ref[:, cols], preferred_element_type=F32)
        part += jnp.dot(low, high_ref[:, cols], preferred_element_type=F32)
        for c in range(9):
            out_ref[:, c * LAGS + j * 256:c * LAGS + j * 256 + 256] = part[c * 16:c * 16 + 16]
    for f in range(2):
        pltpu.make_async_copy(pack.at[f, rest], pack.at[f, rest], send_sem.at[f]).wait()
    pltpu.make_async_copy(lout.at[lrest], lout.at[lrest], lsend_sem).wait()
    pltpu.make_async_copy(cross.at[orest], cross.at[orest], osend_sem).wait()


def mine_rows(mine):
    return pl.ds(pl.multiple_of(mine * 8, 8), RR)


def correlate(spectra, lists):
    vmem = pl.BlockSpec(memory_space=pltpu.VMEM)
    sem = pltpu.SemaphoreType
    return pl.pallas_call(
        correlate_kernel,
        out_shape=jax.ShapeDtypeStruct((16, 9 * LAGS), F32),
        in_specs=[vmem, vmem],
        out_specs=vmem,
        scratch_shapes=[
            pltpu.VMEM((6, HS * STB, BINS), F32), pltpu.VMEM((2, ND * 8, 128), F32), pltpu.VMEM((2, ND * 8, 128), F32),
            pltpu.VMEM((NT, 2, 128), I32), pltpu.VMEM((128, 128), F32), pltpu.VMEM((8, 8, 128), F32),
            pltpu.VMEM((32, 1024, 256), BF16), pltpu.VMEM((384, 1024), BF16), pltpu.VMEM((2, 192, 256), F32),
            pltpu.VMEM((32, 24, 128), F32), pltpu.VMEM((ND * 8, 128), F32), pltpu.VMEM((ND * 8, 128), F32),
            pltpu.VMEM((2 * BINS, LAGS), BF16), pltpu.VMEM((2 * BINS, LAGS), BF16), pltpu.VMEM((2, 32, LAGS), F32),
            pltpu.VMEM((144, 2 * BINS), F32), sem.REGULAR, sem.REGULAR, sem.DMA((2,)), sem.DMA((2,)), sem.DMA((2,)),
            sem.DMA, sem.DMA, sem.DMA, sem.DMA, sem.DMA, sem.DMA],
        compiler_params=pltpu.CompilerParams(collective_id=0, has_side_effects=True, vmem_limit_bytes=60 * 2**20),
        name="correlate",
    )(spectra, lists)


def body(spectra, send_list, pair_list, pair_count):
    pairs = pair_list[0]
    live = jnp.arange(pairs.shape[0], dtype=I32)[:, None] < pair_count[0]
    slots = jnp.where(live, pairs, -1).T.reshape(128)
    lists = jnp.stack([send_list[0].reshape(128), slots])
    return correlate(spectra, lists)


def solution(mesh):
    in_specs = (P("hour", None, "tile", None), P("tile", None, None), P("tile", None, None), P("tile"))
    return jax.shard_map(body, mesh=mesh, in_specs=in_specs, out_specs=P(("tile", "hour"), None), check_vma=False)
```

```python
import functools
import math

import jax
import jax.numpy as jnp
from jax import lax
from jax.experimental import pallas as pl
from jax.experimental.pallas import tpu as pltpu
from jax.sharding import PartitionSpec as P

MESH = pl.DeviceIdType.MESH
F32, BF16, I32 = jnp.float32, jnp.bfloat16, jnp.int32

NFFT = 2048
LAGS = 1024
BINS = 512
SEGS = 32
HS = 8
STB = 16
NT, NH = 64, 4
ND = NT * NH
CH = 12
RR = 3


def position():
    t = lax.axis_index("tile")
    return t, lax.axis_index("hour"), t // 8, t % 8


def entry_barrier():
    t, h, z, xc = position()
    bar = pltpu.get_barrier_semaphore()
    for i in range(1, 8):
        pl.semaphore_signal(bar, inc=1, device_id=(((z + i) % 8) * 8 + xc, h), device_id_type=MESH)
    for i in range(1, 8):
        pl.semaphore_signal(bar, inc=1, device_id=(z * 8 + (xc + i) % 8, h), device_id_type=MESH)
    for i in range(1, NH):
        pl.semaphore_signal(bar, inc=1, device_id=(t, (h + i) % NH), device_id_type=MESH)


def barrier_rounds(plane_sem, all_sem, plane_act, act):
    t, h, z, xc = position()
    pl.semaphore_wait(pltpu.get_barrier_semaphore(), 17)
    others = [z * 8 + (xc + i) % 8 for i in range(1, 8)]
    for t2 in others:
        pl.semaphore_signal(plane_sem, inc=1, device_id=(t2, h), device_id_type=MESH)
    near = [(z + d) % 8 * 8 + xc for d in (4, 3, 5, 2, 6, 1, 7)] + others
    for one in (plane_act, act):
        for t2 in near:
            one(t2, h)
    for i in range(1, NH):
        act(t, (h + i) % NH)
    pl.semaphore_wait(plane_sem, 7)
    for i in range(1, NH):
        pl.semaphore_signal(all_sem, inc=1, device_id=(t, (h + i) % NH), device_id_type=MESH)
    zs = [((z + d) % 8) * 8 for d in (4, 3, 5, 2, 6, 1, 7, 0)]

    for one in (plane_act, act):
        def plane(i, carry, one=one):
            xc2 = (xc + i) % 8
            for base in zs[:7]:
                one(base + xc2, h)
            return carry

        lax.fori_loop(1, 8, plane, 0)
    pl.semaphore_wait(all_sem, NH - 1)

    def rest(k, carry):
        xc2, h2 = (xc + k) % 8, (h + k // 8) % NH
        for n, base in enumerate(zs):
            if n < 7:
                act(base + xc2, h2)
            else:
                pl.when(k % 8 > 0)(lambda: act(base + xc2, h2))
        return carry

    lax.fori_loop(8, 8 * NH, rest, 0)


def each_peer(planes, act):
    t, h, z, xc = position()
    zs = [((z + d) % 8) * 8 for d in range(8)]
    cs = [(xc + d) % 2 for d in range(2)]

    def some(k, carry):
        x2, h2 = ((xc // 2 + k) % 4) * 2, (h + k // 4) % NH
        for dz in range(8):
            for dc in range(2):
                if dz + dc == 0:
                    pl.when(k > 0)(lambda: act(zs[0] + x2 + cs[0], h2))
                else:
                    act(zs[dz] + x2 + cs[dc], h2)
        return carry

    lax.fori_loop(0, 4 * planes, some, 0)


def roll(x, shift, axis):
    return pltpu.roll(x, shift, axis)


def swap_blocks(x):
    sub = lax.broadcasted_iota(I32, (8, 128), 0)
    lane = lax.broadcasted_iota(I32, (8, 128), 1)
    for b in (1, 2, 4):
        step = 16 * b
        sb = (sub & b) != 0
        lb = (lane & step) != 0
        down = roll(roll(x, 8 - b, 0), step, 1)
        up = roll(roll(x, b, 0), 128 - step, 1)
        x = jnp.where(sb == lb, x, jnp.where(sb, up, down))
    return x


def lag_tables(high_ref, low_ref, fine_ref):
    scale = 1.0 / math.sqrt(BINS * SEGS)
    lag = lax.broadcasted_iota(I32, (32, LAGS), 1) - LAGS // 2
    fine = ((lax.broadcasted_iota(I32, (32, LAGS), 0) * lag) & (NFFT - 1)).astype(F32) * (2.0 * math.pi / NFFT)
    fine_ref[0] = jnp.cos(fine)
    fine_ref[1] = jnp.sin(fine)
    lag1 = lax.broadcasted_iota(I32, (8, LAGS), 1) - LAGS // 2

    def rows(a, carry):
        coarse = ((lag1 * (32 * a)) & (NFFT - 1)).astype(F32) * (2.0 * math.pi / NFFT)
        cosine, sine = jnp.cos(coarse)[0:1] * scale, jnp.sin(coarse)[0:1] * scale
        at = pl.multiple_of(a % 8 * 32, 32)
        for part, value in ((0, cosine * fine_ref[0] - sine * fine_ref[1]),
                            (256, -(sine * fine_ref[0] + cosine * fine_ref[1]))):
            high = value.astype(BF16)
            high_ref[a // 8, pl.ds(part + at, 32), :] = high
            low_ref[a // 8, pl.ds(part + at, 32), :] = (value - high.astype(F32)).astype(BF16)
        return carry

    lax.fori_loop(0, BINS // 32, rows, 0)


def rows_of(d, n):
    return pl.ds(pl.multiple_of(d * 8, 8), n)


def whiten_all(spec_ref, white):
    lane = lax.broadcasted_iota(I32, (STB, BINS), 1)

    def one(s, carry):
        x = spec_ref[s]
        power = jnp.sum(x * x, axis=0)
        total = power
        total += jnp.where(lane >= 1, roll(power, 1, 1), 0.0)
        total += jnp.where(lane >= 2, roll(power, 2, 1), 0.0)
        total += jnp.where(lane < BINS - 1, roll(power, BINS - 1, 1), 0.0)
        total += jnp.where(lane < BINS - 2, roll(power, BINS - 2, 1), 0.0)
        water = jnp.sum(power, axis=1, keepdims=True) * (1.0 / (3.0 * BINS))
        inv = 1.0 / jnp.sqrt(total * (1.0 / 15.0) + 0.25 * water + 1e-06)
        white[:, pl.ds(pl.multiple_of(s * STB, STB), STB), :] = x * inv[None]
        return carry

    lax.fori_loop(0, HS, one, 0)


def pack_bin(f, white, pack):
    for c in range(6):
        for half in range(2):
            cols = slice((2 * f + half) * 128, (2 * f + half) * 128 + 128)
            pack[f, pl.ds(half * 1024 + c, 128, stride=8), :] = white[c, :, cols].T


def pack_lists(send_ref, pair_ref, count_ref, lists):
    live = lax.broadcasted_iota(I32, (2, 64), 1) < count_ref[0]
    pairs = jnp.where(live, pair_ref[...], -1)
    sends = send_ref[...]
    for j in range(2):
        lists[0:1, j * 64:j * 64 + 64] = sends[j:j + 1]
        lists[1:2, j * 64:j * 64 + 64] = pairs[j:j + 1]


def resolve_stations(lout_ref, slots_ref, idx_ref):
    sends = lout_ref[:, 0, :].astype(F32)
    slots_ref[...] = jnp.concatenate([sends, jnp.zeros((64, 128), F32)], axis=0).T
    first, second = slots_ref[0:NT, :], slots_ref[NT:2 * NT, :]
    slot = lout_ref[:, 1, :]
    owner = jnp.maximum(slot, 0) // 2
    pick = jnp.where(slot % 2 == 0, jnp.take_along_axis(first, owner, axis=1),
                     jnp.take_along_axis(second, owner, axis=1))
    station = owner.astype(F32) * STB + pick
    station = jnp.where((slot < 0) | (pick >= STB), -1.0, station)
    for tg in range(8):
        idx_ref[tg] = swap_blocks(station[tg * 8:(tg + 1) * 8])


def build_selectors(idx_ref, hot):
    station = lax.broadcasted_iota(I32, (128, 256), 0)

    def one(i, carry):
        tg, h = i // NH, i % NH
        wanted = jnp.concatenate([idx_ref[tg, pl.ds(h, 1), :], idx_ref[tg, pl.ds(4 + h, 1), :]], axis=1).astype(I32)
        for k in range(8):
            hot[i, k * 128:k * 128 + 128, :] = (station == wanted - k * 128).astype(F32).astype(BF16)
        return carry

    lax.fori_loop(0, 32, one, 0)


def build_table(f, recv, table):
    sub = lax.broadcasted_iota(I32, (8, 128), 0)
    lane = lax.broadcasted_iota(I32, (8, 128), 1)
    l16, l32, l64 = (lane & 16) != 0, (lane & 32) != 0, (lane & 64) != 0
    same, top = ((sub & 4) != 0) == l16, (sub & 4) != 0

    def one(og):
        for ci in range(3):
            parts = []
            for c in (2 * ci, 2 * ci + 1):
                v = []
                for g in range(4):
                    x = recv[f, pl.ds(og * 256 + g * 64 + c, 8, stride=8), :]
                    y = roll(x, 4, 0)
                    v.append(jnp.where(same, x, jnp.where(top, roll(y, 112, 1), roll(y, 16, 1))))
                w = [None] * 4
                for hi in range(2):
                    a, b = v[2 * hi], v[2 * hi + 1]
                    w[2 * hi] = jnp.where(l32, roll(b, 32, 1), a)
                    w[2 * hi + 1] = jnp.where(l32, b, roll(a, 96, 1))
                u = [None] * 4
                for lo in range(2):
                    a, b = w[lo], w[2 + lo]
                    u[lo] = jnp.where(l64, roll(b, 64, 1), a)
                    u[2 + lo] = jnp.where(l64, b, roll(a, 64, 1))
                parts.append(u)
            for sv in range(4):
                both = jnp.concatenate([parts[0][sv], parts[1][sv]], axis=0)
                high = both.astype(BF16)
                low = (both - high.astype(F32)).astype(BF16)
                row = (sv * 6 + 2 * ci) * 8
                cols = pl.ds(pl.multiple_of(og * 128, 128), 128)
                table[row:row + 16, cols] = high
                table[192 + row:192 + row + 16, cols] = low

    def some(k, carry):
        for j in range(4):
            one(4 * k + j)
        return carry

    lax.fori_loop(0, 2, some, 0)


def select_pairs(table, chosen, prod):
    full = jnp.dot(table[...], chosen, preferred_element_type=F32)
    prod[...] = full[:192] + full[192:]


def pair_sums(prod):
    acc = [None] * 18
    for sv in range(4):
        rows = [slice((sv * 6 + c) * 8, (sv * 6 + c) * 8 + 8) for c in range(6)]
        a = [prod[r, 0:128] for r in rows]
        b = [prod[r, 128:256] for r in rows]
        for p in range(3):
            for q in range(3):
                re = a[2 * p] * b[2 * q] + a[2 * p + 1] * b[2 * q + 1]
                im = a[2 * p + 1] * b[2 * q] - a[2 * p] * b[2 * q + 1]
                n = (p * 3 + q) * 2
                acc[n] = re if sv == 0 else acc[n] + re
                acc[n + 1] = im if sv == 0 else acc[n + 1] + im
    return [jnp.sum(v, axis=0, keepdims=True) for v in acc]


def block_at(i):
    _, h, z, _ = position()
    return (z + 3 * (i + 1)) % 8, (h + i // 8 + 1) % NH


def correlate_kernel(spec_hbm, slist_ref, plist_ref, count_ref, out_ref, spec_ref, lists_ref, white, pack, recv, lout, slots_ref, idx_ref, hot, table, prod0, prod1,
                     cross, got, high_ref, low_ref, fine_ref, sum_ref, plane_sem, all_sem, send_sem, recv_sem, own_sem,
                     lsend_sem, lrecv_sem, lown_sem, osend_sem, orecv_sem, oown_sem, fetch_sem):
    t, h, _, _ = position()
    me, mine = t * NH + h, h * NT + t
    fetch = pltpu.make_async_copy(spec_hbm, spec_ref, fetch_sem)
    fetch.start()
    entry_barrier()
    pack_lists(slist_ref, plist_ref, count_ref, lists_ref)
    fetch.wait()
    whiten_all(spec_ref, white)
    pack_bin(0, white, pack)
    owns = [pltpu.make_async_copy(pack.at[f, rows_of(mine, 6)], recv.at[f, rows_of(me, 6)], own_sem.at[f])
            for f in range(2)]

    def send(f, t2, h2):
        pltpu.make_async_remote_copy(src_ref=pack.at[f, rows_of(h2 * NT + t2, 6)], dst_ref=recv.at[f, rows_of(me, 6)],
                                     send_sem=send_sem.at[f], recv_sem=recv_sem.at[f], device_id=(t2, h2),
                                     device_id_type=MESH).start()

    def send_lists(t2, h2):
        pltpu.make_async_remote_copy(src_ref=lists_ref, dst_ref=lout.at[t], send_sem=lsend_sem, recv_sem=lrecv_sem,
                                     device_id=(t2, h2), device_id_type=MESH).start()

    barrier_rounds(plane_sem, all_sem, send_lists, functools.partial(send, 0))
    lown = pltpu.make_async_copy(lists_ref, lout.at[t], lown_sem)
    lown.start()
    owns[0].start()
    pack_bin(1, white, pack)
    owns[1].start()
    each_peer(NH, functools.partial(send, 1))
    lag_tables(high_ref, low_ref, fine_ref)
    lown.wait()
    lrest = pl.ds(0, NT - 1)
    pltpu.make_async_copy(lout.at[lrest], lout.at[lrest], lrecv_sem).wait()
    resolve_stations(lout, slots_ref, idx_ref)
    build_selectors(idx_ref, hot)
    rest = pl.ds(0, (ND - 1) * 6)

    def arrived(f):
        owns[f].wait()
        pltpu.make_async_copy(recv.at[f, rest], recv.at[f, rest], recv_sem.at[f]).wait()
        build_table(f, recv, table)

    def place(i):
        tg, h2 = block_at(i)
        return tg * NH + h2

    def deliver(f, i, last=False):
        tg, h2 = block_at(i)
        for x in range(8):
            t2 = tg * 8 + x
            src, dst = cross.at[f, rows_of(h2 * NT + t2, RR)], got.at[f, rows_of(mine, RR)]
            copy = pltpu.make_async_remote_copy(src_ref=src, dst_ref=dst, send_sem=osend_sem.at[f],
                                                recv_sem=orecv_sem.at[f], device_id=(t2, h2), device_id_type=MESH)
            if last:
                pl.when(t2 != t)(copy.start)
            else:
                copy.start()

    def finish(f, i, sums):
        tg, h2 = block_at(i)
        zero = jnp.zeros((6, 128), F32)
        for r in range(RR):
            part = jnp.concatenate(sums[r * 8:r * 8 + 8] if r < 2 else sums[16:18] + [zero], axis=0)
            cross[f, pl.ds((h2 * NT + tg * 8) * 8 + r, 8, stride=8), :] = swap_blocks(part)

    def blocks(f):
        select_pairs(table, hot[place(0)], prod0)

        def two(k, carry):
            i = 2 * k
            select_pairs(table, hot[place(i + 1)], prod1)
            finish(f, i, pair_sums(prod0))
            select_pairs(table, hot[place(jnp.minimum(i + 2, 31))], prod0)
            finish(f, i + 1, pair_sums(prod1))
            deliver(f, i)
            pl.when(k < 15)(lambda: deliver(f, i + 1))
            return carry

        lax.fori_loop(0, 16, two, 0)
        deliver(f, 31, last=True)
        pltpu.make_async_copy(cross.at[f, rows_of(mine, RR)], got.at[f, rows_of(mine, RR)], oown_sem.at[f]).start()

    orest = pl.ds(0, (ND - 1) * RR)

    def transform(f):
        pltpu.make_async_copy(cross.at[f, rows_of(mine, RR)], got.at[f, rows_of(mine, RR)], oown_sem.at[f]).wait()
        pltpu.make_async_copy(got.at[f, orest], got.at[f, orest], orecv_sem.at[f]).wait()
        for r in range(RR):
            turned = got[f, pl.ds(r, ND, stride=8), :].T
            for g in range(8 if r < 2 else 2):
                c, ri = (r * 8 + g) // 2, g % 2
                sum_ref[c * 16:c * 16 + 16, ri * 256:ri * 256 + 256] = turned[g * 16:g * 16 + 16]
        total = sum_ref[...]
        high = total.astype(BF16)
        low = (total - high.astype(F32)).astype(BF16)
        for j in range(4):
            cols = slice(j * 256, j * 256 + 256)
            wh, wl = high_ref[f, :, cols], low_ref[f, :, cols]
            part = jnp.dot(high, wh, preferred_element_type=F32)
            part += jnp.dot(high, wl, preferred_element_type=F32)
            part += jnp.dot(low, wh, preferred_element_type=F32)
            for c in range(9):
                at = slice(c * LAGS + j * 256, c * LAGS + j * 256 + 256)
                piece = part[c * 16:c * 16 + 16]
                out_ref[:, at] = piece if f == 0 else out_ref[:, at] + piece

    arrived(0)
    blocks(0)
    arrived(1)
    blocks(1)
    transform(0)
    transform(1)
    for f in range(2):
        pltpu.make_async_copy(pack.at[f, rest], pack.at[f, rest], send_sem.at[f]).wait()
        pltpu.make_async_copy(cross.at[f, orest], cross.at[f, orest], osend_sem.at[f]).wait()
    pltpu.make_async_copy(lout.at[lrest], lout.at[lrest], lsend_sem).wait()


def correlate(spectra, send_list, pair_list, pair_count):
    vmem = pl.BlockSpec(memory_space=pltpu.VMEM)
    sem = pltpu.SemaphoreType
    return pl.pallas_call(
        correlate_kernel,
        out_shape=jax.ShapeDtypeStruct((16, 9 * LAGS), F32),
        in_specs=[pl.BlockSpec(memory_space=pl.ANY), vmem, vmem, pl.BlockSpec(memory_space=pltpu.SMEM)],
        out_specs=vmem,
        scratch_shapes=[
            pltpu.VMEM((HS, 6, STB, BINS), F32), pltpu.VMEM((2, 128), I32),
            pltpu.VMEM((6, HS * STB, BINS), F32), pltpu.VMEM((2, ND * 8, 128), F32), pltpu.VMEM((2, ND * 8, 128), F32),
            pltpu.VMEM((NT, 2, 128), I32), pltpu.VMEM((128, 128), F32), pltpu.VMEM((8, 8, 128), F32),
            pltpu.VMEM((32, 1024, 256), BF16), pltpu.VMEM((384, 1024), BF16), pltpu.VMEM((192, 256), F32), pltpu.VMEM((192, 256), F32),
            pltpu.VMEM((2, ND * 8, 128), F32), pltpu.VMEM((2, ND * 8, 128), F32),
            pltpu.VMEM((2, BINS, LAGS), BF16), pltpu.VMEM((2, BINS, LAGS), BF16), pltpu.VMEM((2, 32, LAGS), F32),
            pltpu.VMEM((144, BINS), F32), sem.REGULAR, sem.REGULAR, sem.DMA((2,)), sem.DMA((2,)), sem.DMA((2,)),
            sem.DMA, sem.DMA, sem.DMA, sem.DMA((2,)), sem.DMA((2,)), sem.DMA((2,)), sem.DMA],
        compiler_params=pltpu.CompilerParams(collective_id=0, has_side_effects=True, vmem_limit_bytes=60 * 2**20),
        name="correlate",
    )(spectra, send_list, pair_list, pair_count)


def body(spectra, send_list, pair_list, pair_count):
    return correlate(spectra, send_list[0].T, pair_list[0].T, pair_count)


def solution(mesh):
    in_specs = (P("hour", None, "tile", None), P("tile", None, None), P("tile", None, None), P("tile"))
    return jax.shard_map(body, mesh=mesh, in_specs=in_specs, out_specs=P(("tile", "hour"), None), check_vma=False)
```

```python
import functools
import math

import jax
import jax.numpy as jnp
from jax import lax
from jax.experimental import pallas as pl
from jax.experimental.pallas import tpu as pltpu
from jax.sharding import PartitionSpec as P

MESH = pl.DeviceIdType.MESH
F32, BF16, I32 = jnp.float32, jnp.bfloat16, jnp.int32

NFFT = 2048
LAGS = 1024
BINS = 512
SEGS = 32
HS = 8
STB = 16
NT, NH = 64, 4
ND = NT * NH
CH = 12
UNROLL = 4
RR = 3


def position():
    t = lax.axis_index("tile")
    return t, lax.axis_index("hour"), t // 8, t % 8


def entry_barrier():
    t, h, z, xc = position()
    bar = pltpu.get_barrier_semaphore()
    for i in range(1, 8):
        pl.semaphore_signal(bar, inc=1, device_id=(((z + i) % 8) * 8 + xc, h), device_id_type=MESH)
    for i in range(1, 8):
        pl.semaphore_signal(bar, inc=1, device_id=(z * 8 + (xc + i) % 8, h), device_id_type=MESH)
    for i in range(1, NH):
        pl.semaphore_signal(bar, inc=1, device_id=(t, (h + i) % NH), device_id_type=MESH)


def barrier_rounds(plane_sem, all_sem, plane_act, act):
    t, h, z, xc = position()
    pl.semaphore_wait(pltpu.get_barrier_semaphore(), 17)
    others = [z * 8 + (xc + i) % 8 for i in range(1, 8)]
    for t2 in others:
        pl.semaphore_signal(plane_sem, inc=1, device_id=(t2, h), device_id_type=MESH)
    near = [(z + d) % 8 * 8 + xc for d in (4, 3, 5, 2, 6, 1, 7)] + others
    for one in (plane_act, act):
        for t2 in near:
            one(t2, h)
    for i in range(1, NH):
        act(t, (h + i) % NH)
    pl.semaphore_wait(plane_sem, 7)
    for i in range(1, NH):
        pl.semaphore_signal(all_sem, inc=1, device_id=(t, (h + i) % NH), device_id_type=MESH)
    zs = [((z + d) % 8) * 8 for d in (4, 3, 5, 2, 6, 1, 7, 0)]

    for one in (plane_act, act):
        def plane(i, carry, one=one):
            xc2 = (xc + i) % 8
            for base in zs[:7]:
                one(base + xc2, h)
            return carry

        lax.fori_loop(1, 8, plane, 0)
    pl.semaphore_wait(all_sem, NH - 1)

    def rest(k, carry):
        xc2, h2 = (xc + k) % 8, (h + k // 8) % NH
        for n, base in enumerate(zs):
            if n < 7:
                act(base + xc2, h2)
            else:
                pl.when(k % 8 > 0)(lambda: act(base + xc2, h2))
        return carry

    lax.fori_loop(8, 8 * NH, rest, 0)


def each_peer(planes, act):
    t, h, z, xc = position()
    zs = [((z + d) % 8) * 8 for d in range(8)]
    cs = [(xc + d) % 2 for d in range(2)]

    def some(k, carry):
        x2, h2 = ((xc // 2 + k) % 4) * 2, (h + k // 4) % NH
        for dz in range(8):
            for dc in range(2):
                if dz + dc == 0:
                    pl.when(k > 0)(lambda: act(zs[0] + x2 + cs[0], h2))
                else:
                    act(zs[dz] + x2 + cs[dc], h2)
        return carry

    lax.fori_loop(0, 4 * planes, some, 0)


def roll(x, shift, axis):
    return pltpu.roll(x, shift, axis)


def swap_blocks(x):
    sub = lax.broadcasted_iota(I32, (8, 128), 0)
    lane = lax.broadcasted_iota(I32, (8, 128), 1)
    for b in (1, 2, 4):
        step = 16 * b
        sb = (sub & b) != 0
        lb = (lane & step) != 0
        down = roll(roll(x, 8 - b, 0), step, 1)
        up = roll(roll(x, b, 0), 128 - step, 1)
        x = jnp.where(sb == lb, x, jnp.where(sb, up, down))
    return x


def lag_tables(high_ref, low_ref, fine_ref):
    scale = 1.0 / math.sqrt(BINS * SEGS)
    lag = lax.broadcasted_iota(I32, (32, LAGS), 1) - LAGS // 2
    fine = ((lax.broadcasted_iota(I32, (32, LAGS), 0) * lag) & (NFFT - 1)).astype(F32) * (2.0 * math.pi / NFFT)
    fine_ref[0] = jnp.cos(fine)
    fine_ref[1] = jnp.sin(fine)
    lag1 = lax.broadcasted_iota(I32, (8, LAGS), 1) - LAGS // 2

    def rows(a, carry):
        coarse = ((lag1 * (32 * a)) & (NFFT - 1)).astype(F32) * (2.0 * math.pi / NFFT)
        cosine, sine = jnp.cos(coarse)[0:1] * scale, jnp.sin(coarse)[0:1] * scale
        at = pl.multiple_of(a % 8 * 32, 32)
        for part, value in ((0, cosine * fine_ref[0] - sine * fine_ref[1]),
                            (256, -(sine * fine_ref[0] + cosine * fine_ref[1]))):
            high = value.astype(BF16)
            high_ref[a // 8, pl.ds(part + at, 32), :] = high
            low_ref[a // 8, pl.ds(part + at, 32), :] = (value - high.astype(F32)).astype(BF16)
        return carry

    lax.fori_loop(0, BINS // 32, rows, 0)


def rows_of(d, n):
    return pl.ds(pl.multiple_of(d * 8, 8), n)


def whiten_all(spec_ref, white):
    lane = lax.broadcasted_iota(I32, (STB, BINS), 1)

    def one(s, carry):
        x = spec_ref[s]
        power = jnp.sum(x * x, axis=0)
        total = power
        total += jnp.where(lane >= 1, roll(power, 1, 1), 0.0)
        total += jnp.where(lane >= 2, roll(power, 2, 1), 0.0)
        total += jnp.where(lane < BINS - 1, roll(power, BINS - 1, 1), 0.0)
        total += jnp.where(lane < BINS - 2, roll(power, BINS - 2, 1), 0.0)
        water = jnp.sum(power, axis=1, keepdims=True) * (1.0 / (3.0 * BINS))
        inv = 1.0 / jnp.sqrt(total * (1.0 / 15.0) + 0.25 * water + 1e-06)
        white[:, pl.ds(pl.multiple_of(s * STB, STB), STB), :] = x * inv[None]
        return carry

    lax.fori_loop(0, HS, one, 0)


def pack_bin(f, white, pack):
    for c in range(6):
        for half in range(2):
            cols = slice((2 * f + half) * 128, (2 * f + half) * 128 + 128)
            pack[f, pl.ds(half * 1024 + c, 128, stride=8), :] = white[c, :, cols].T


def pack_lists(send_ref, pair_ref, count_ref, lists):
    live = lax.broadcasted_iota(I32, (2, 64), 1) < count_ref[0]
    pairs = jnp.where(live, pair_ref[...], -1)
    sends = send_ref[...]
    for j in range(2):
        lists[0:1, j * 64:j * 64 + 64] = sends[j:j + 1]
        lists[1:2, j * 64:j * 64 + 64] = pairs[j:j + 1]


def resolve_stations(lout_ref, slots_ref, idx_ref):
    sends = lout_ref[:, 0, :].astype(F32)
    slots_ref[...] = jnp.concatenate([sends, jnp.zeros((64, 128), F32)], axis=0).T
    first, second = slots_ref[0:NT, :], slots_ref[NT:2 * NT, :]
    slot = lout_ref[:, 1, :]
    owner = jnp.maximum(slot, 0) // 2
    pick = jnp.where(slot % 2 == 0, jnp.take_along_axis(first, owner, axis=1),
                     jnp.take_along_axis(second, owner, axis=1))
    station = owner.astype(F32) * STB + pick
    station = jnp.where((slot < 0) | (pick >= STB), -1.0, station)
    for tg in range(8):
        idx_ref[tg] = swap_blocks(station[tg * 8:(tg + 1) * 8])


def build_selectors(idx_ref, hot):
    station = lax.broadcasted_iota(I32, (128, 256), 0)

    def one(i, carry):
        tg, h = i // NH, i % NH
        wanted = jnp.concatenate([idx_ref[tg, pl.ds(h, 1), :], idx_ref[tg, pl.ds(4 + h, 1), :]], axis=1).astype(I32)
        for k in range(8):
            hot[i, k * 128:k * 128 + 128, :] = (station == wanted - k * 128).astype(F32).astype(BF16)
        return carry

    lax.fori_loop(0, 32, one, 0)


def build_table(f, recv, table):
    sub = lax.broadcasted_iota(I32, (8, 128), 0)
    lane = lax.broadcasted_iota(I32, (8, 128), 1)
    l16, l32, l64 = (lane & 16) != 0, (lane & 32) != 0, (lane & 64) != 0
    same, top = ((sub & 4) != 0) == l16, (sub & 4) != 0

    def one(og):
        for ci in range(3):
            parts = []
            for c in (2 * ci, 2 * ci + 1):
                v = []
                for g in range(4):
                    x = recv[f, pl.ds(og * 256 + g * 64 + c, 8, stride=8), :]
                    y = roll(x, 4, 0)
                    v.append(jnp.where(same, x, jnp.where(top, roll(y, 112, 1), roll(y, 16, 1))))
                w = [None] * 4
                for hi in range(2):
                    a, b = v[2 * hi], v[2 * hi + 1]
                    w[2 * hi] = jnp.where(l32, roll(b, 32, 1), a)
                    w[2 * hi + 1] = jnp.where(l32, b, roll(a, 96, 1))
                u = [None] * 4
                for lo in range(2):
                    a, b = w[lo], w[2 + lo]
                    u[lo] = jnp.where(l64, roll(b, 64, 1), a)
                    u[2 + lo] = jnp.where(l64, b, roll(a, 64, 1))
                parts.append(u)
            for sv in range(4):
                both = jnp.concatenate([parts[0][sv], parts[1][sv]], axis=0)
                high = both.astype(BF16)
                low = (both - high.astype(F32)).astype(BF16)
                row = (sv * 6 + 2 * ci) * 8
                cols = pl.ds(pl.multiple_of(og * 128, 128), 128)
                table[row:row + 16, cols] = high
                table[192 + row:192 + row + 16, cols] = low

    def some(k, carry):
        for j in range(4):
            one(4 * k + j)
        return carry

    lax.fori_loop(0, 2, some, 0)


def select_pairs(table, chosen, prod):
    full = jnp.dot(table[...], chosen, preferred_element_type=F32)
    prod[...] = full[:192] + full[192:]


def pair_sums(prod):
    acc = [None] * 18
    for sv in range(4):
        rows = [slice((sv * 6 + c) * 8, (sv * 6 + c) * 8 + 8) for c in range(6)]
        a = [prod[r, 0:128] for r in rows]
        b = [prod[r, 128:256] for r in rows]
        for p in range(3):
            for q in range(3):
                re = a[2 * p] * b[2 * q] + a[2 * p + 1] * b[2 * q + 1]
                im = a[2 * p + 1] * b[2 * q] - a[2 * p] * b[2 * q + 1]
                n = (p * 3 + q) * 2
                acc[n] = re if sv == 0 else acc[n] + re
                acc[n + 1] = im if sv == 0 else acc[n + 1] + im
    return [jnp.sum(v, axis=0, keepdims=True) for v in acc]


def block_at(i):
    _, h, z, _ = position()
    return (z + 3 * (i + 1)) % 8, (h + i // 8 + 1) % NH


def correlate_kernel(spec_hbm, slist_ref, plist_ref, count_ref, out_ref, spec_ref, lists_ref, white, pack, recv, lout, slots_ref, idx_ref, hot, table, prod0, prod1,
                     cross, got, high_ref, low_ref, fine_ref, sum_ref, plane_sem, all_sem, send_sem, recv_sem, own_sem,
                     lsend_sem, lrecv_sem, lown_sem, osend_sem, orecv_sem, oown_sem, fetch_sem):
    t, h, _, _ = position()
    me, mine = t * NH + h, h * NT + t
    fetch = pltpu.make_async_copy(spec_hbm, spec_ref, fetch_sem)
    fetch.start()
    entry_barrier()
    pack_lists(slist_ref, plist_ref, count_ref, lists_ref)
    fetch.wait()
    whiten_all(spec_ref, white)
    pack_bin(0, white, pack)
    owns = [pltpu.make_async_copy(pack.at[f, rows_of(mine, 6)], recv.at[f, rows_of(me, 6)], own_sem.at[f])
            for f in range(2)]

    def send(f, t2, h2):
        pltpu.make_async_remote_copy(src_ref=pack.at[f, rows_of(h2 * NT + t2, 6)], dst_ref=recv.at[f, rows_of(me, 6)],
                                     send_sem=send_sem.at[f], recv_sem=recv_sem.at[f], device_id=(t2, h2),
                                     device_id_type=MESH).start()

    def send_lists(t2, h2):
        pltpu.make_async_remote_copy(src_ref=lists_ref, dst_ref=lout.at[t], send_sem=lsend_sem, recv_sem=lrecv_sem,
                                     device_id=(t2, h2), device_id_type=MESH).start()

    barrier_rounds(plane_sem, all_sem, send_lists, functools.partial(send, 0))
    lown = pltpu.make_async_copy(lists_ref, lout.at[t], lown_sem)
    lown.start()
    owns[0].start()
    pack_bin(1, white, pack)
    owns[1].start()
    each_peer(NH, functools.partial(send, 1))
    lag_tables(high_ref, low_ref, fine_ref)
    lown.wait()
    lrest = pl.ds(0, NT - 1)
    pltpu.make_async_copy(lout.at[lrest], lout.at[lrest], lrecv_sem).wait()
    resolve_stations(lout, slots_ref, idx_ref)
    build_selectors(idx_ref, hot)
    rest = pl.ds(0, (ND - 1) * 6)

    def arrived(f):
        owns[f].wait()
        pltpu.make_async_copy(recv.at[f, rest], recv.at[f, rest], recv_sem.at[f]).wait()
        build_table(f, recv, table)

    def place(i):
        tg, h2 = block_at(i)
        return tg * NH + h2

    def deliver(f, i, last=False):
        tg, h2 = block_at(i)
        for x in range(8):
            t2 = tg * 8 + x
            src, dst = cross.at[f, rows_of(h2 * NT + t2, RR)], got.at[f, rows_of(mine, RR)]
            copy = pltpu.make_async_remote_copy(src_ref=src, dst_ref=dst, send_sem=osend_sem.at[f],
                                                recv_sem=orecv_sem.at[f], device_id=(t2, h2), device_id_type=MESH)
            if last:
                pl.when(t2 != t)(copy.start)
            else:
                copy.start()

    def finish(f, i, sums):
        tg, h2 = block_at(i)
        zero = jnp.zeros((6, 128), F32)
        for r in range(RR):
            part = jnp.concatenate(sums[r * 8:r * 8 + 8] if r < 2 else sums[16:18] + [zero], axis=0)
            cross[f, pl.ds((h2 * NT + tg * 8) * 8 + r, 8, stride=8), :] = swap_blocks(part)

    def blocks(f):
        prods = (prod0, prod1)

        def some(i, last=False):
            for j in range(UNROLL):
                if not last or j < UNROLL - 1:
                    select_pairs(table, hot[place(i + j + 1)], prods[(j + 1) % 2])
                finish(f, i + j, pair_sums(prods[j % 2]))
            for j in range(UNROLL):
                deliver(f, i + j, last and j == UNROLL - 1)

        def step(k, carry):
            some(UNROLL * k)
            return carry

        select_pairs(table, hot[place(0)], prod0)
        lax.fori_loop(0, 32 // UNROLL - 1, step, 0)
        some(32 - UNROLL, last=True)
        pltpu.make_async_copy(cross.at[f, rows_of(mine, RR)], got.at[f, rows_of(mine, RR)], oown_sem.at[f]).start()

    orest = pl.ds(0, (ND - 1) * RR)

    def transform(f):
        pltpu.make_async_copy(cross.at[f, rows_of(mine, RR)], got.at[f, rows_of(mine, RR)], oown_sem.at[f]).wait()
        pltpu.make_async_copy(got.at[f, orest], got.at[f, orest], orecv_sem.at[f]).wait()
        for r in range(RR):
            turned = got[f, pl.ds(r, ND, stride=8), :].T
            for g in range(8 if r < 2 else 2):
                c, ri = (r * 8 + g) // 2, g % 2
                sum_ref[c * 16:c * 16 + 16, ri * 256:ri * 256 + 256] = turned[g * 16:g * 16 + 16]
        total = sum_ref[...]
        high = total.astype(BF16)
        low = (total - high.astype(F32)).astype(BF16)
        for j in range(4):
            cols = slice(j * 256, j * 256 + 256)
            wh, wl = high_ref[f, :, cols], low_ref[f, :, cols]
            part = jnp.dot(high, wh, preferred_element_type=F32)
            part += jnp.dot(high, wl, preferred_element_type=F32)
            part += jnp.dot(low, wh, preferred_element_type=F32)
            for c in range(9):
                at = slice(c * LAGS + j * 256, c * LAGS + j * 256 + 256)
                piece = part[c * 16:c * 16 + 16]
                out_ref[:, at] = piece if f == 0 else out_ref[:, at] + piece

    arrived(0)
    blocks(0)
    arrived(1)
    blocks(1)
    transform(0)
    transform(1)
    for f in range(2):
        pltpu.make_async_copy(pack.at[f, rest], pack.at[f, rest], send_sem.at[f]).wait()
        pltpu.make_async_copy(cross.at[f, orest], cross.at[f, orest], osend_sem.at[f]).wait()
    pltpu.make_async_copy(lout.at[lrest], lout.at[lrest], lsend_sem).wait()


def correlate(spectra, send_list, pair_list, pair_count):
    vmem = pl.BlockSpec(memory_space=pltpu.VMEM)
    sem = pltpu.SemaphoreType
    return pl.pallas_call(
        correlate_kernel,
        out_shape=pltpu.VMEM((16, 9 * LAGS), F32),
        in_specs=[pl.BlockSpec(memory_space=pl.ANY), vmem, vmem, pl.BlockSpec(memory_space=pltpu.SMEM)],
        out_specs=vmem,
        scratch_shapes=[
            pltpu.VMEM((HS, 6, STB, BINS), F32), pltpu.VMEM((2, 128), I32),
            pltpu.VMEM((6, HS * STB, BINS), F32), pltpu.VMEM((2, ND * 8, 128), F32), pltpu.VMEM((2, ND * 8, 128), F32),
            pltpu.VMEM((NT, 2, 128), I32), pltpu.VMEM((128, 128), F32), pltpu.VMEM((8, 8, 128), F32),
            pltpu.VMEM((32, 1024, 256), BF16), pltpu.VMEM((384, 1024), BF16), pltpu.VMEM((192, 256), F32), pltpu.VMEM((192, 256), F32),
            pltpu.VMEM((2, ND * 8, 128), F32), pltpu.VMEM((2, ND * 8, 128), F32),
            pltpu.VMEM((2, BINS, LAGS), BF16), pltpu.VMEM((2, BINS, LAGS), BF16), pltpu.VMEM((2, 32, LAGS), F32),
            pltpu.VMEM((144, BINS), F32), sem.REGULAR, sem.REGULAR, sem.DMA((2,)), sem.DMA((2,)), sem.DMA((2,)),
            sem.DMA, sem.DMA, sem.DMA, sem.DMA((2,)), sem.DMA((2,)), sem.DMA((2,)), sem.DMA],
        compiler_params=pltpu.CompilerParams(collective_id=0, has_side_effects=True, vmem_limit_bytes=60 * 2**20),
        name="correlate",
    )(spectra, send_list, pair_list, pair_count)


def body(spectra, send_list, pair_list, pair_count):
    return correlate(spectra, send_list[0].T, pair_list[0].T, pair_count)


def solution(mesh):
    in_specs = (P("hour", None, "tile", None), P("tile", None, None), P("tile", None, None), P("tile"))
    return jax.shard_map(body, mesh=mesh, in_specs=in_specs, out_specs=P(("tile", "hour"), None), check_vma=False)
```

```python
import functools
import math

import jax
import jax.numpy as jnp
from jax import lax
from jax.experimental import pallas as pl
from jax.experimental.pallas import tpu as pltpu
from jax.sharding import PartitionSpec as P

MESH = pl.DeviceIdType.MESH
F32, BF16, I32, F8 = jnp.float32, jnp.bfloat16, jnp.int32, jnp.float8_e5m2
LOW = 2.0 ** 22

NFFT = 2048
LAGS = 1024
BINS = 512
SEGS = 32
HS = 8
STB = 16
NT, NH = 64, 4
ND = NT * NH
CH = 12
UNROLL = 4
RR = 3


def position():
    t = lax.axis_index("tile")
    return t, lax.axis_index("hour"), t // 8, t % 8


def entry_barrier():
    t, h, z, xc = position()
    bar = pltpu.get_barrier_semaphore()
    for i in range(1, 8):
        pl.semaphore_signal(bar, inc=1, device_id=(((z + i) % 8) * 8 + xc, h), device_id_type=MESH)
    for i in range(1, 8):
        pl.semaphore_signal(bar, inc=1, device_id=(z * 8 + (xc + i) % 8, h), device_id_type=MESH)
    for i in range(1, NH):
        pl.semaphore_signal(bar, inc=1, device_id=(t, (h + i) % NH), device_id_type=MESH)


def barrier_rounds(plane_sem, all_sem, plane_act, act):
    t, h, z, xc = position()
    pl.semaphore_wait(pltpu.get_barrier_semaphore(), 17)
    others = [z * 8 + (xc + i) % 8 for i in range(1, 8)]
    for t2 in others:
        pl.semaphore_signal(plane_sem, inc=1, device_id=(t2, h), device_id_type=MESH)
    near = [(z + d) % 8 * 8 + xc for d in (4, 3, 5, 2, 6, 1, 7)] + others
    for one in (plane_act, act):
        for t2 in near:
            one(t2, h)
    for i in range(1, NH):
        act(t, (h + i) % NH)
    pl.semaphore_wait(plane_sem, 7)
    for i in range(1, NH):
        pl.semaphore_signal(all_sem, inc=1, device_id=(t, (h + i) % NH), device_id_type=MESH)
    zs = [((z + d) % 8) * 8 for d in (4, 3, 5, 2, 6, 1, 7, 0)]

    for one in (plane_act, act):
        def plane(i, carry, one=one):
            xc2 = (xc + i) % 8
            for base in zs[:7]:
                one(base + xc2, h)
            return carry

        lax.fori_loop(1, 8, plane, 0)
    pl.semaphore_wait(all_sem, NH - 1)

    def rest(k, carry):
        xc2, h2 = (xc + k) % 8, (h + k // 8) % NH
        for n, base in enumerate(zs):
            if n < 7:
                act(base + xc2, h2)
            else:
                pl.when(k % 8 > 0)(lambda: act(base + xc2, h2))
        return carry

    lax.fori_loop(8, 8 * NH, rest, 0)


def each_peer(planes, act):
    t, h, z, xc = position()
    zs = [((z + d) % 8) * 8 for d in range(8)]
    cs = [(xc + d) % 2 for d in range(2)]

    def some(k, carry):
        x2, h2 = ((xc // 2 + k) % 4) * 2, (h + k // 4) % NH
        for dz in range(8):
            for dc in range(2):
                if dz + dc == 0:
                    pl.when(k > 0)(lambda: act(zs[0] + x2 + cs[0], h2))
                else:
                    act(zs[dz] + x2 + cs[dc], h2)
        return carry

    lax.fori_loop(0, 4 * planes, some, 0)


def roll(x, shift, axis):
    return pltpu.roll(x, shift, axis)


def swap_blocks(x):
    sub = lax.broadcasted_iota(I32, (8, 128), 0)
    lane = lax.broadcasted_iota(I32, (8, 128), 1)
    for b in (1, 2, 4):
        step = 16 * b
        sb = (sub & b) != 0
        lb = (lane & step) != 0
        down = roll(roll(x, 8 - b, 0), step, 1)
        up = roll(roll(x, b, 0), 128 - step, 1)
        x = jnp.where(sb == lb, x, jnp.where(sb, up, down))
    return x


def lag_tables(high_ref, low_ref, fine_ref):
    scale = 1.0 / math.sqrt(BINS * SEGS)
    lag = lax.broadcasted_iota(I32, (32, LAGS), 1) - LAGS // 2
    fine = ((lax.broadcasted_iota(I32, (32, LAGS), 0) * lag) & (NFFT - 1)).astype(F32) * (2.0 * math.pi / NFFT)
    fine_ref[0] = jnp.cos(fine)
    fine_ref[1] = jnp.sin(fine)
    lag1 = lax.broadcasted_iota(I32, (8, LAGS), 1) - LAGS // 2

    def rows(a, carry):
        coarse = ((lag1 * (32 * a)) & (NFFT - 1)).astype(F32) * (2.0 * math.pi / NFFT)
        cosine, sine = jnp.cos(coarse)[0:1] * scale, jnp.sin(coarse)[0:1] * scale
        at = pl.multiple_of(a % 8 * 32, 32)
        for part, value in ((0, cosine * fine_ref[0] - sine * fine_ref[1]),
                            (256, -(sine * fine_ref[0] + cosine * fine_ref[1]))):
            high = value.astype(BF16)
            high_ref[a // 8, pl.ds(part + at, 32), :] = high
            low_ref[a // 8, pl.ds(part + at, 32), :] = (value - high.astype(F32)).astype(BF16)
        return carry

    lax.fori_loop(0, BINS // 32, rows, 0)


def rows_of(d, n):
    return pl.ds(pl.multiple_of(d * 8, 8), n)


def whiten_all(spec_ref, white):
    lane = lax.broadcasted_iota(I32, (STB, BINS), 1)

    def one(s, carry):
        x = spec_ref[s]
        power = jnp.sum(x * x, axis=0)
        total = power
        total += jnp.where(lane >= 1, roll(power, 1, 1), 0.0)
        total += jnp.where(lane >= 2, roll(power, 2, 1), 0.0)
        total += jnp.where(lane < BINS - 1, roll(power, BINS - 1, 1), 0.0)
        total += jnp.where(lane < BINS - 2, roll(power, BINS - 2, 1), 0.0)
        water = jnp.sum(power, axis=1, keepdims=True) * (1.0 / (3.0 * BINS))
        inv = 1.0 / jnp.sqrt(total * (1.0 / 15.0) + 0.25 * water + 1e-06)
        white[:, pl.ds(pl.multiple_of(s * STB, STB), STB), :] = x * inv[None]
        return carry

    lax.fori_loop(0, HS, one, 0)


def pack_bin(f, white, pack):
    for c in range(6):
        for half in range(2):
            cols = slice((2 * f + half) * 128, (2 * f + half) * 128 + 128)
            pack[f, pl.ds(half * 1024 + c, 128, stride=8), :] = white[c, :, cols].T


def pack_lists(send_ref, pair_ref, count_ref, lists):
    live = lax.broadcasted_iota(I32, (2, 64), 1) < count_ref[0]
    pairs = jnp.where(live, pair_ref[...], -1)
    sends = send_ref[...]
    for j in range(2):
        lists[0:1, j * 64:j * 64 + 64] = sends[j:j + 1]
        lists[1:2, j * 64:j * 64 + 64] = pairs[j:j + 1]


def resolve_stations(lout_ref, slots_ref, idx_ref):
    sends = lout_ref[:, 0, :].astype(F32)
    slots_ref[...] = jnp.concatenate([sends, jnp.zeros((64, 128), F32)], axis=0).T
    first, second = slots_ref[0:NT, :], slots_ref[NT:2 * NT, :]
    slot = lout_ref[:, 1, :]
    owner = jnp.maximum(slot, 0) // 2
    pick = jnp.where(slot % 2 == 0, jnp.take_along_axis(first, owner, axis=1),
                     jnp.take_along_axis(second, owner, axis=1))
    station = owner.astype(F32) * STB + pick
    station = jnp.where((slot < 0) | (pick >= STB), -1.0, station)
    for tg in range(8):
        idx_ref[tg] = swap_blocks(station[tg * 8:(tg + 1) * 8])


def build_selectors(idx_ref, hot, hot8):
    station = lax.broadcasted_iota(I32, (128, 256), 0)

    def one(i, carry):
        tg, h = i // NH, i % NH
        wanted = jnp.concatenate([idx_ref[tg, pl.ds(h, 1), :], idx_ref[tg, pl.ds(4 + h, 1), :]], axis=1).astype(I32)
        for k in range(8):
            one_hot = (station == wanted - k * 128).astype(F32)
            hot[i, k * 128:k * 128 + 128, :] = one_hot.astype(BF16)
            hot8[i, k * 128:k * 128 + 128, :] = one_hot.astype(F8)
        return carry

    lax.fori_loop(0, 32, one, 0)


def build_table(f, recv, table, low_table):
    sub = lax.broadcasted_iota(I32, (8, 128), 0)
    lane = lax.broadcasted_iota(I32, (8, 128), 1)
    l16, l32, l64 = (lane & 16) != 0, (lane & 32) != 0, (lane & 64) != 0
    same, top = ((sub & 4) != 0) == l16, (sub & 4) != 0

    def one(og):
        for ci in range(3):
            parts = []
            for c in (2 * ci, 2 * ci + 1):
                v = []
                for g in range(4):
                    x = recv[f, pl.ds(og * 256 + g * 64 + c, 8, stride=8), :]
                    y = roll(x, 4, 0)
                    v.append(jnp.where(same, x, jnp.where(top, roll(y, 112, 1), roll(y, 16, 1))))
                w = [None] * 4
                for hi in range(2):
                    a, b = v[2 * hi], v[2 * hi + 1]
                    w[2 * hi] = jnp.where(l32, roll(b, 32, 1), a)
                    w[2 * hi + 1] = jnp.where(l32, b, roll(a, 96, 1))
                u = [None] * 4
                for lo in range(2):
                    a, b = w[lo], w[2 + lo]
                    u[lo] = jnp.where(l64, roll(b, 64, 1), a)
                    u[2 + lo] = jnp.where(l64, b, roll(a, 64, 1))
                parts.append(u)
            for sv in (0, 2):
                both = jnp.concatenate([parts[0][sv], parts[1][sv], parts[0][sv + 1], parts[1][sv + 1]], axis=0)
                high = both.astype(BF16)
                row = ci * 64 + sv * 16
                cols = slice(og * 128, og * 128 + 128)
                table[row:row + 32, cols] = high
                low_table[row:row + 32, cols] = ((both - high.astype(F32)) * LOW).astype(F8)

    for og in range(8):
        one(og)


def select_pairs(table, low_table, chosen, chosen8, prod):
    high = jnp.dot(table[...], chosen, preferred_element_type=F32)
    prod[...] = high + jnp.dot(low_table[...], chosen8, preferred_element_type=F32) * (1.0 / LOW)


def pair_sums(prod):
    acc = [None] * 18
    for sv in range(4):
        rows = [slice(c // 2 * 64 + sv * 16 + c % 2 * 8, c // 2 * 64 + sv * 16 + c % 2 * 8 + 8) for c in range(6)]
        a = [prod[r, 0:128] for r in rows]
        b = [prod[r, 128:256] for r in rows]
        for p in range(3):
            for q in range(3):
                re = a[2 * p] * b[2 * q] + a[2 * p + 1] * b[2 * q + 1]
                im = a[2 * p + 1] * b[2 * q] - a[2 * p] * b[2 * q + 1]
                n = (p * 3 + q) * 2
                acc[n] = re if sv == 0 else acc[n] + re
                acc[n + 1] = im if sv == 0 else acc[n + 1] + im
    return [jnp.sum(v, axis=0, keepdims=True) for v in acc]


def block_at(i):
    _, h, z, _ = position()
    return (z + 3 * (i + 1)) % 8, (h + i // 8 + 1) % NH


def correlate_kernel(spec_hbm, slist_ref, plist_ref, count_ref, out_ref, spec_ref, lists_ref, white, pack, recv, lout, slots_ref, idx_ref, hot, hot8, table, low_table, prod0, prod1,
                     cross, got, high_ref, low_ref, fine_ref, sum_ref, plane_sem, all_sem, send_sem, recv_sem, own_sem,
                     lsend_sem, lrecv_sem, lown_sem, osend_sem, orecv_sem, oown_sem, fetch_sem):
    t, h, _, _ = position()
    me, mine = t * NH + h, h * NT + t
    fetch = pltpu.make_async_copy(spec_hbm, spec_ref, fetch_sem)
    fetch.start()
    entry_barrier()
    pack_lists(slist_ref, plist_ref, count_ref, lists_ref)
    fetch.wait()
    whiten_all(spec_ref, white)
    pack_bin(0, white, pack)
    owns = [pltpu.make_async_copy(pack.at[f, rows_of(mine, 6)], recv.at[f, rows_of(me, 6)], own_sem.at[f])
            for f in range(2)]

    def send(f, t2, h2):
        pltpu.make_async_remote_copy(src_ref=pack.at[f, rows_of(h2 * NT + t2, 6)], dst_ref=recv.at[f, rows_of(me, 6)],
                                     send_sem=send_sem.at[f], recv_sem=recv_sem.at[f], device_id=(t2, h2),
                                     device_id_type=MESH).start()

    def send_lists(t2, h2):
        pltpu.make_async_remote_copy(src_ref=lists_ref, dst_ref=lout.at[t], send_sem=lsend_sem, recv_sem=lrecv_sem,
                                     device_id=(t2, h2), device_id_type=MESH).start()

    barrier_rounds(plane_sem, all_sem, send_lists, functools.partial(send, 0))
    lown = pltpu.make_async_copy(lists_ref, lout.at[t], lown_sem)
    lown.start()
    owns[0].start()
    pack_bin(1, white, pack)
    owns[1].start()
    each_peer(NH, functools.partial(send, 1))
    lag_tables(high_ref, low_ref, fine_ref)
    lown.wait()
    lrest = pl.ds(0, NT - 1)
    pltpu.make_async_copy(lout.at[lrest], lout.at[lrest], lrecv_sem).wait()
    resolve_stations(lout, slots_ref, idx_ref)
    build_selectors(idx_ref, hot, hot8)
    rest = pl.ds(0, (ND - 1) * 6)

    def arrived(f):
        owns[f].wait()
        pltpu.make_async_copy(recv.at[f, rest], recv.at[f, rest], recv_sem.at[f]).wait()
        build_table(f, recv, table, low_table)

    def place(i):
        tg, h2 = block_at(i)
        return tg * NH + h2

    def deliver(f, i, last=False):
        tg, h2 = block_at(i)
        for x in range(8):
            t2 = tg * 8 + x
            src, dst = cross.at[f, rows_of(h2 * NT + t2, RR)], got.at[f, rows_of(mine, RR)]
            copy = pltpu.make_async_remote_copy(src_ref=src, dst_ref=dst, send_sem=osend_sem.at[f],
                                                recv_sem=orecv_sem.at[f], device_id=(t2, h2), device_id_type=MESH)
            if last:
                pl.when(t2 != t)(copy.start)
            else:
                copy.start()

    def finish(f, i, sums):
        tg, h2 = block_at(i)
        zero = jnp.zeros((6, 128), F32)
        for r in range(RR):
            part = jnp.concatenate(sums[r * 8:r * 8 + 8] if r < 2 else sums[16:18] + [zero], axis=0)
            cross[f, pl.ds((h2 * NT + tg * 8) * 8 + r, 8, stride=8), :] = swap_blocks(part)

    def blocks(f):
        prods = (prod0, prod1)

        def some(i, last=False):
            for j in range(UNROLL):
                if not last or j < UNROLL - 1:
                    select_pairs(table, low_table, hot[place(i + j + 1)], hot8[place(i + j + 1)], prods[(j + 1) % 2])
                finish(f, i + j, pair_sums(prods[j % 2]))
            for j in range(UNROLL):
                deliver(f, i + j, last and j == UNROLL - 1)

        def step(k, carry):
            some(UNROLL * k)
            return carry

        select_pairs(table, low_table, hot[place(0)], hot8[place(0)], prod0)
        lax.fori_loop(0, 32 // UNROLL - 1, step, 0)
        some(32 - UNROLL, last=True)
        pltpu.make_async_copy(cross.at[f, rows_of(mine, RR)], got.at[f, rows_of(mine, RR)], oown_sem.at[f]).start()

    orest = pl.ds(0, (ND - 1) * RR)

    def transform(f):
        pltpu.make_async_copy(cross.at[f, rows_of(mine, RR)], got.at[f, rows_of(mine, RR)], oown_sem.at[f]).wait()
        pltpu.make_async_copy(got.at[f, orest], got.at[f, orest], orecv_sem.at[f]).wait()
        for r in range(RR):
            turned = got[f, pl.ds(r, ND, stride=8), :].T
            for g in range(8 if r < 2 else 2):
                c, ri = (r * 8 + g) // 2, g % 2
                sum_ref[c * 16:c * 16 + 16, ri * 256:ri * 256 + 256] = turned[g * 16:g * 16 + 16]
        total = sum_ref[...]
        high = total.astype(BF16)
        low = (total - high.astype(F32)).astype(BF16)
        for j in range(4):
            cols = slice(j * 256, j * 256 + 256)
            wh, wl = high_ref[f, :, cols], low_ref[f, :, cols]
            part = jnp.dot(high, wh, preferred_element_type=F32)
            part += jnp.dot(high, wl, preferred_element_type=F32)
            part += jnp.dot(low, wh, preferred_element_type=F32)
            for c in range(9):
                at = slice(c * LAGS + j * 256, c * LAGS + j * 256 + 256)
                piece = part[c * 16:c * 16 + 16]
                out_ref[:, at] = piece if f == 0 else out_ref[:, at] + piece

    arrived(0)
    blocks(0)
    arrived(1)
    blocks(1)
    transform(0)
    transform(1)
    for f in range(2):
        pltpu.make_async_copy(pack.at[f, rest], pack.at[f, rest], send_sem.at[f]).wait()
        pltpu.make_async_copy(cross.at[f, orest], cross.at[f, orest], osend_sem.at[f]).wait()
    pltpu.make_async_copy(lout.at[lrest], lout.at[lrest], lsend_sem).wait()


def correlate(spectra, send_list, pair_list, pair_count):
    vmem = pl.BlockSpec(memory_space=pltpu.VMEM)
    sem = pltpu.SemaphoreType
    return pl.pallas_call(
        correlate_kernel,
        out_shape=pltpu.VMEM((16, 9 * LAGS), F32),
        in_specs=[pl.BlockSpec(memory_space=pl.ANY), vmem, vmem, pl.BlockSpec(memory_space=pltpu.SMEM)],
        out_specs=vmem,
        scratch_shapes=[
            pltpu.VMEM((HS, 6, STB, BINS), F32), pltpu.VMEM((2, 128), I32),
            pltpu.VMEM((6, HS * STB, BINS), F32), pltpu.VMEM((2, ND * 8, 128), F32), pltpu.VMEM((2, ND * 8, 128), F32),
            pltpu.VMEM((NT, 2, 128), I32), pltpu.VMEM((128, 128), F32), pltpu.VMEM((8, 8, 128), F32),
            pltpu.VMEM((32, 1024, 256), BF16), pltpu.VMEM((32, 1024, 256), F8), pltpu.VMEM((192, 1024), BF16), pltpu.VMEM((192, 1024), F8), pltpu.VMEM((192, 256), F32), pltpu.VMEM((192, 256), F32),
            pltpu.VMEM((2, ND * 8, 128), F32), pltpu.VMEM((2, ND * 8, 128), F32),
            pltpu.VMEM((2, BINS, LAGS), BF16), pltpu.VMEM((2, BINS, LAGS), BF16), pltpu.VMEM((2, 32, LAGS), F32),
            pltpu.VMEM((144, BINS), F32), sem.REGULAR, sem.REGULAR, sem.DMA((2,)), sem.DMA((2,)), sem.DMA((2,)),
            sem.DMA, sem.DMA, sem.DMA, sem.DMA((2,)), sem.DMA((2,)), sem.DMA((2,)), sem.DMA],
        compiler_params=pltpu.CompilerParams(collective_id=0, has_side_effects=True, vmem_limit_bytes=60 * 2**20),
        name="correlate",
    )(spectra, send_list, pair_list, pair_count)


def body(spectra, send_list, pair_list, pair_count):
    return correlate(spectra, send_list[0].T, pair_list[0].T, pair_count)


def solution(mesh):
    in_specs = (P("hour", None, "tile", None), P("tile", None, None), P("tile", None, None), P("tile"))
    return jax.shard_map(body, mesh=mesh, in_specs=in_specs, out_specs=P(("tile", "hour"), None), check_vma=False)
```
